128 devices in a mesh: dom: 16 (over x, y_lo, core), blk: 8 (over z, y_hi).
Axes of the slice: x: 4, y: 4 (y_hi: 2, y_lo: 2; y = y_hi * 2 + y_lo), z: 4, core: 2. Of those that a mesh axis runs over, the one named last changes fastest.
Arguments:
- positions: float32 [3, 262144], P(None, ('dom', 'blk')), may hold values from -0.5 to 0.5
- strength: float32 [3, 262144], P(None, ('dom', 'blk')), may hold values from -0.18 to 0.18
- core_radius: float32 [262144], P(('dom', 'blk')), may hold values from 0.15 to 0.3
- dye_amount: float32 [262144], P(('dom', 'blk')), may hold values from -0.18 to 0.18
- cell_fraction: float32 [3, 262144], P(None, ('dom', 'blk')), may hold values from 0 to 1
- cell_index: int32 [262144], P(('dom', 'blk')), may hold values from 0 to 127
- tile_local: int32 [262144], P(('dom', 'blk')), may hold values from 0 to 15
- owner_dom: int32 [262144, 1], P(('dom', 'blk')), may hold values from 0 to 15; in each aligned block of 2048 rows (0 to 2047, 2048 to 4095, ...) at most 640 rows name the same one
Outputs:
- velocity: float32 [3, 262144], P(None, ('dom', 'blk'))
- tile_grid: float32 [2048, 4, 128], P(('dom', 'blk'))
The draws below stay inside these ranges and needn't reach their ends.
Inputs may be any that keep to these rules, and one draw needn't show every extreme that they name: `owner_dom`: in every block of 2048 rows of one device no value appears more than 640 times, and in some block a value appears exactly 640 times.
All inputs are finite; a program needn't handle non-finite values.
Results may differ from the reference program's by a relative error of at most 0.0003.
Values sent between devices are 32-bit elements; how exact they have to be, the bound alone decides.
A program may use at most 64 MiB of HBM per device.

```python
import math
import jax
import jax.numpy as jnp
import numpy as np
from jax import lax

PD = 2048
P_SIZE = 262144
REGION = 16384
TPD = 16
TILES = 2048
CAP = 640
N_DOM = 16
N_BLK = 8


def with_ends(array, stream_key, low, high):
    shape = array.shape
    place = [jax.random.randint(jax.random.fold_in(stream_key, axis), (), 0, shape[axis]) for axis in range(len(shape))]
    array = array.at[tuple(place)].set(low)
    longest = shape.index(max(shape))
    place[longest] = (place[longest] + 1) % shape[longest]
    return array.at[tuple(place)].set(high)


def level_of(rng, dims, cuts, least, largest):
    factor_of, own = 1.0, jax.random.fold_in(rng, 6)
    for dim, blocks in cuts:
        heights = jnp.exp(jax.random.uniform(jax.random.fold_in(own, dim), (blocks,), jnp.float32, least / len(cuts), largest / len(cuts)))
        factor_of = factor_of * jnp.repeat(heights, dims[dim] // blocks).reshape([-1 if axis == dim else 1 for axis in range(len(dims))])
    return factor_of


def routed_block(stream_key, own, number, rows, number_of, top, limit, skew):
    order = jax.random.permutation(stream_key, number_of)
    packed, common = shares(number_of, rows * top, limit, skew, True), shares(number_of, rows * top, limit, skew, False)
    places = jnp.arange(number_of)

    def named(tallies, offset_by):
        used = int((tallies > 0).sum())
        fixed = max(1, used // 4)
        moved = fixed + (places - fixed + offset_by * (used - fixed)) % max(1, number_of - fixed)
        return jnp.zeros((number_of,), jnp.int32).at[order[jnp.where(places < fixed, places, moved)]].set(jnp.asarray(tallies, jnp.int32))

    tallies = jnp.where(number % 4 == 0, named(packed, number // 4), named(common, number - number // 4 - 1))
    mixed = jax.random.permutation(jax.random.fold_in(own, 3), number_of)
    donor, sink = mixed[0:number_of // 2 * 2:2], mixed[1:number_of // 2 * 2:2]
    room = jnp.minimum(tallies[donor] - 1, limit - tallies[sink]) // 2
    room = jnp.where((donor == order[0]) | (sink == order[0]) | (tallies[sink] == 0), 0, jnp.maximum(room, 0))
    moved = jax.random.randint(jax.random.fold_in(own, 4), (number_of // 2,), 0, 1 << 20) % (room + 1)
    tallies = tallies.at[donor].add(-moved).at[sink].add(moved)
    items = jnp.searchsorted(jnp.cumsum(tallies), jnp.arange(rows * top), side="right").astype(jnp.int32)
    table = items.reshape(top, rows).T
    table = table[jax.random.permutation(jax.random.fold_in(own, 1), rows)]
    offset_by = jax.random.randint(jax.random.fold_in(own, 2), (rows, 1), 0, top)
    return jnp.take_along_axis(table, (jnp.arange(top)[None, :] + offset_by) % top, axis=1)


def shares(number_of, total, reach, slope, full):
    weights = [(1 << 20) // math.isqrt(rank ** slope) + 1 for rank in range(1, number_of + 1)]
    largest = reach if full else min(reach, max(-(-total // number_of), total * weights[0] // sum(weights)))
    least = 1 if total - largest >= number_of - 1 else 0
    counts, spare = [largest] + [least] * (number_of - 1), total - largest - least * (number_of - 1)
    while spare > 0:
        free = [i for i in range(1, number_of) if counts[i] < largest] or [i for i in range(1, number_of) if counts[i] < reach]
        pool, budget = sum([weights[i] for i in free]), spare
        for i in free:
            extra = min(reach - counts[i], max(1, budget * weights[i] // pool), spare)
            counts[i] = counts[i] + extra
            spare = spare - extra
    return np.array(counts)


def centred(key, extent, deviation, bound, cuts=(), kind=jnp.bfloat16):
    array = jax.random.normal(key, extent, jnp.float32) * deviation
    if len(cuts) > 0:
        array = level_of(key, extent, cuts, -0.22, 0.18) * array
    return jnp.clip(array, min=-bound, max=bound).astype(kind)


def setup_inputs(seed: int = 0) -> dict:
    keys = jax.random.split(jax.random.key(seed), 9)
    positions = jnp.clip(jax.random.uniform(keys[0], (3, P_SIZE), jnp.float32, -0.5, 0.5) * level_of(keys[0], (3, P_SIZE), ((1, 128),), -0.4, 0.0), -0.5, 0.5)
    strength = centred(keys[1], (3, P_SIZE), 0.03, 0.18, ((1, 128),), jnp.float32)
    core_radius = jnp.clip(jnp.exp(math.log(0.3) - 0.6931472 * jax.random.uniform(keys[2], (P_SIZE,), jnp.float32) ** level_of(keys[2], (P_SIZE,), ((0, 128),), -0.2, 0.2)), 0.15, 0.3)
    dye_amount = centred(keys[3], (P_SIZE,), 0.03, 0.18, ((0, 128),), jnp.float32)
    cell_fraction = jnp.clip(1.0 * jax.random.uniform(keys[4], (3, P_SIZE), jnp.float32) ** level_of(keys[4], (3, P_SIZE), ((1, 128),), -0.2, 0.2), 0.0, 1.0)
    cell_index = with_ends(jax.random.randint(keys[5], (P_SIZE,), 0, 128), jax.random.fold_in(keys[5], 1), 0, 127).astype(jnp.int32)
    tile_local = with_ends(jax.random.randint(keys[6], (P_SIZE,), 0, TPD), jax.random.fold_in(keys[6], 1), 0, TPD - 1).astype(jnp.int32)
    owner_dom_keys = jax.random.split(jax.random.fold_in(keys[7], 1), P_SIZE // PD)
    owner_dom_turns = jax.random.permutation(jax.random.fold_in(keys[7], 3), P_SIZE // PD)
    owner_dom = jax.vmap(lambda own, number: routed_block(jax.random.fold_in(keys[7], 2), own, number, PD, N_DOM, 1, CAP, 3))(owner_dom_keys, owner_dom_turns).reshape((P_SIZE, 1))
    return dict(positions=positions, strength=strength, core_radius=core_radius, dye_amount=dye_amount, cell_fraction=cell_fraction, cell_index=cell_index, tile_local=tile_local, owner_dom=owner_dom)


time_step = 0.02
move_scale = 2.0
inverse_volume = 32.0
kernel_scale = 1.0 / (4.0 * math.pi)
highest = lax.Precision.HIGHEST

def cross_product(left_vec, right_vec):
    return jnp.stack([left_vec[1] * right_vec[2] - left_vec[2] * right_vec[1], left_vec[2] * right_vec[0] - left_vec[0] * right_vec[2], left_vec[0] * right_vec[1] - left_vec[1] * right_vec[0]])

def pair_sums(partial_value, source_block, target_rows):
    points = source_block[0:3]
    vortex = source_block[3:6]
    radius = source_block[6]
    source_rows = jnp.concatenate([-2.0 * points, (lax.optimization_barrier(jnp.sum(points * points, axis=0)) + radius * radius)[None], jnp.ones_like(radius)[None]], axis=0)
    square = lax.dot_general(source_rows, target_rows, (((0,), (0,)), ((), ())), precision=highest, preferred_element_type=jnp.float32)
    inverse = lax.rsqrt(square)
    kernel_vals = kernel_scale * inverse * inverse * inverse
    slope_vals = -3.0 * kernel_vals * inverse * inverse
    crossed = cross_product(vortex, points)
    moment_one = (points[:, None, :] * vortex[None, :, :]).reshape(9, -1)
    moment_two = (points[:, None, :] * crossed[None, :, :]).reshape(9, -1)
    first_rows = jnp.concatenate([vortex, crossed], axis=0)
    second_rows = jnp.concatenate([vortex, crossed, moment_one, moment_two], axis=0)
    first = partial_value[0] + jnp.dot(first_rows, kernel_vals, precision=highest, preferred_element_type=jnp.float32)
    second = partial_value[1] + jnp.dot(second_rows, slope_vals, precision=highest, preferred_element_type=jnp.float32)
    return (first, second)

def block_fold(running, sources, target_rows):
    overall = sources.shape[1]
    block_width = math.gcd(overall, 1024)
    blocks = sources.reshape(7, overall // block_width, block_width).transpose(1, 0, 2)

    def scan_step(partial_value, source_block):
        return (pair_sums(partial_value, source_block, target_rows), None)
    result, ignored = lax.scan(scan_step, running, blocks)
    return result

def target_rows_of(points):
    return jnp.concatenate([points, jnp.ones_like(points[0])[None], lax.optimization_barrier(jnp.sum(points * points, axis=0))[None]], axis=0)

def combine(points, vortex, first, second):
    sum_kernel = first[0:3]
    velocity = cross_product(sum_kernel, points) - first[3:6]
    term_one = cross_product(sum_kernel, vortex)
    moment_one = second[6:15].reshape(3, 3, -1)
    moment_two = second[15:24].reshape(3, 3, -1)
    dot_self = lax.optimization_barrier(jnp.sum(vortex * points, axis=0))
    mixed_one = lax.optimization_barrier(jnp.sum(vortex[:, None, :] * moment_one, axis=0))
    mixed_two = lax.optimization_barrier(jnp.sum(vortex[:, None, :] * moment_two, axis=0))
    term_two = dot_self * (cross_product(second[0:3], points) - second[3:6]) - cross_product(mixed_one, points) + mixed_two
    return (velocity, term_one + term_two)

def spline_weight(distance):
    return jnp.where(distance < 1.0, 1.0 - 2.5 * distance * distance + 1.5 * distance * distance * distance, 0.5 * (2.0 - distance) * (2.0 - distance) * (1.0 - distance))

def grid_place(cell_fraction, cell_index, velocity):
    cell_start = jnp.stack([cell_index % 8, cell_index // 8 % 4, cell_index // 32]).astype(jnp.float32)
    coords = cell_start + cell_fraction + move_scale * velocity
    lowest = jnp.floor(coords)
    fraction = coords - lowest
    lowest_int = lowest.astype(jnp.int32)
    base_code = lowest_int[2] % 4 * 32 + lowest_int[1] % 4 * 8 + lowest_int[0] % 8
    return (fraction, base_code)

def node_weights(fraction):
    per_axis = [[spline_weight(fraction[axis_id] + 1.0), spline_weight(fraction[axis_id]), spline_weight(1.0 - fraction[axis_id]), spline_weight(2.0 - fraction[axis_id])] for axis_id in range(3)]
    weights = []
    for along_z in range(4):
        for along_y in range(4):
            for along_x in range(4):
                weights.append(per_axis[2][along_z] * per_axis[1][along_y] * per_axis[0][along_x])
    return jnp.stack(weights)

def cells_of(base_code):
    base_x = base_code % 8
    base_y = base_code // 8 % 4
    base_z = base_code // 32
    stencil_cells = []
    for along_z in range(4):
        for along_y in range(4):
            for along_x in range(4):
                stencil_cells.append((base_z + along_z - 1) % 4 * 32 + (base_y + along_y - 1) % 4 * 8 + (base_x + along_x - 1) % 8)
    return jnp.stack(stencil_cells)

def spread(weights, stencil_cells):
    cell_ids = jnp.arange(128, dtype=jnp.int32)[:, None]
    overall = jnp.zeros((128, weights.shape[1]), jnp.float32)
    for node in range(64):
        overall = overall + jnp.where(stencil_cells[node][None, :] == cell_ids, weights[node][None, :], 0.0)
    return overall

def reference(positions, strength, core_radius, dye_amount, cell_fraction, cell_index, tile_local, owner_dom):
    sources = jnp.concatenate([positions, strength, core_radius[None]], axis=0)
    regions = sources.reshape(7, N_DOM, REGION).transpose(1, 0, 2)

    def region_work(region_rows):
        points = region_rows[0:3]
        vortex = region_rows[3:6]
        start_sums = (jnp.zeros((6, REGION), jnp.float32), jnp.zeros((24, REGION), jnp.float32))
        first, second = block_fold(start_sums, region_rows, target_rows_of(points))
        return combine(points, vortex, first, second)
    velocity_parts, stretch_parts = lax.map(region_work, regions)
    velocity = velocity_parts.transpose(1, 0, 2).reshape(3, P_SIZE)
    stretch = stretch_parts.transpose(1, 0, 2).reshape(3, P_SIZE)
    new_strength = strength + time_step * stretch
    fraction, base_code = grid_place(cell_fraction, cell_index, velocity)
    block_owner = jnp.arange(P_SIZE, dtype=jnp.int32) // PD % N_BLK
    tile_id = ((owner_dom[:, 0] * N_BLK + block_owner) * TPD + tile_local).astype(jnp.int32)
    values = jnp.concatenate([new_strength, dye_amount[None]], axis=0)
    span = math.gcd(P_SIZE, 16384)
    pieces = P_SIZE // span
    stacked = (values.reshape(4, pieces, span).transpose(1, 0, 2), fraction.reshape(3, pieces, span).transpose(1, 0, 2), base_code.reshape(pieces, span), tile_id.reshape(pieces, span))

    def deposit_step(tile_sums, piece_rows):
        piece_values, piece_fraction, piece_base, piece_tiles = piece_rows
        spread_w = spread(node_weights(piece_fraction), cells_of(piece_base))
        contrib = jnp.einsum('cp,kp->pck', piece_values, spread_w).reshape(-1, 512)
        return (tile_sums + jax.ops.segment_sum(contrib, piece_tiles, num_segments=TILES), None)
    tile_sums, ignored = lax.scan(deposit_step, jnp.zeros((TILES, 512), jnp.float32), stacked)
    tile_grid = (tile_sums * inverse_volume).reshape(TILES, 4, 128)
    return (velocity, tile_grid)
```

```python
import functools
import math

import jax
import jax.numpy as jnp
from jax import lax
from jax.experimental import pallas as pl
from jax.experimental.pallas import tpu as pltpu
from jax.sharding import PartitionSpec as P

MESH = pl.DeviceIdType.MESH
f32, bf16 = jnp.float32, jnp.bfloat16
kernel_scale = 1.0 / (4.0 * math.pi)


def cross_rows(u, v):
    return [u[1] * v[2] - u[2] * v[1], u[2] * v[0] - u[0] * v[2], u[0] * v[1] - u[1] * v[0]]


def split(value, parts):
    pieces = []
    for _ in range(parts):
        piece = value.astype(bf16)
        pieces.append(piece)
        value = value - piece.astype(f32)
    return pieces


def gather_kernel(n, mine_ref, all_ref, send_sems, recv_sems):
    me = lax.axis_index("blk")
    barrier = pltpu.get_barrier_semaphore()
    for step in range(1, n):
        pl.semaphore_signal(barrier, inc=1, device_id={"blk": lax.rem(me + step, n)}, device_id_type=MESH)
    pl.semaphore_wait(barrier, n - 1)
    copies = []
    for step in range(1, n):
        copy = pltpu.make_async_remote_copy(
            src_ref=mine_ref,
            dst_ref=all_ref.at[step],
            send_sem=send_sems.at[step],
            recv_sem=recv_sems.at[step],
            device_id={"blk": lax.rem(me + step, n)},
            device_id_type=MESH,
        )
        copy.start()
        copies.append(copy)
    all_ref[0] = mine_ref[...]
    for copy in copies:
        copy.wait()


def gather(block, n):
    return pl.pallas_call(
        functools.partial(gather_kernel, n),
        out_shape=jax.ShapeDtypeStruct((n,) + block.shape, f32),
        in_specs=[pl.BlockSpec(memory_space=pltpu.VMEM)],
        out_specs=pl.BlockSpec(memory_space=pltpu.VMEM),
        scratch_shapes=[pltpu.SemaphoreType.DMA((n,)), pltpu.SemaphoreType.DMA((n,))],
        compiler_params=pltpu.CompilerParams(collective_id=0, has_side_effects=True),
    )(block)


TT, ST, CH = 256, 512, 64


def pair_kernel(t_ref, s_ref, rk_ref, rg_ref, ok_ref, og_ref, vk0, vk1, vg0, vg1):
    vk, vg = (vk0, vk1), (vg0, vg1)
    count = s_ref.shape[0] // ST
    ok_ref[...] = jnp.zeros_like(ok_ref)
    og_ref[...] = jnp.zeros_like(og_ref)

    def values(targets, index, slot):
        start = pl.multiple_of(index * ST, ST)
        for row in range(0, ST, CH):
            square = jnp.dot(
                s_ref[pl.ds(pl.multiple_of(start + row, CH), CH), :], targets, preferred_element_type=f32
            )
            inverse = lax.rsqrt(square)
            second = inverse * inverse
            kern = second * inverse
            slope = kern * second
            kern_hi = kern.astype(bf16)
            slope_hi = slope.astype(bf16)
            vk[slot][row : row + CH, :] = kern_hi
            vg[slot][row : row + CH, :] = slope_hi
            vk[slot][ST + row : ST + row + CH, :] = (kern - kern_hi.astype(f32)).astype(bf16)
            vg[slot][ST + row : ST + row + CH, :] = (slope - slope_hi.astype(f32)).astype(bf16)

    def sums(at, index, slot):
        start = pl.multiple_of(index * ST, ST)
        rk = rk_ref[:, pl.ds(start, ST)]
        rg = rg_ref[:, pl.ds(start, ST)]
        ok_ref[:, pl.ds(at, TT)] += jnp.dot(
            jnp.concatenate([rk, rk], 1), vk[slot][...], preferred_element_type=f32
        )
        og_ref[:, pl.ds(at, TT)] += jnp.dot(
            jnp.concatenate([rg, rg], 1), vg[slot][...], preferred_element_type=f32
        )

    @pl.loop(0, t_ref.shape[1] // TT)
    def _(tile):
        at = pl.multiple_of(tile * TT, TT)
        targets = t_ref[:, pl.ds(at, TT)]
        values(targets, 0, 0)

        @pl.loop(0, count // 2)
        def _(pair):
            values(targets, 2 * pair + 1, 1)
            sums(at, 2 * pair, 0)
            values(targets, jnp.minimum(2 * pair + 2, count - 1), 0)
            sums(at, 2 * pair + 1, 1)


def pair_sums(targets, sources, kernel_rows, slope_rows):
    local = targets.shape[1]
    return pl.pallas_call(
        pair_kernel,
        out_shape=(
            jax.ShapeDtypeStruct((kernel_rows.shape[0], local), f32),
            jax.ShapeDtypeStruct((slope_rows.shape[0], local), f32),
        ),
        in_specs=[pl.BlockSpec(memory_space=pltpu.VMEM)] * 4,
        out_specs=(pl.BlockSpec(memory_space=pltpu.VMEM),) * 2,
        scratch_shapes=[pltpu.VMEM((2 * ST, TT), bf16)] * 4,
        compiler_params=pltpu.CompilerParams(vmem_limit_bytes=48 << 20),
    )(targets, sources, kernel_rows, slope_rows)


def spline_weight(distance):
    return jnp.where(
        distance < 1.0,
        1.0 - 2.5 * distance * distance + 1.5 * distance * distance * distance,
        0.5 * (2.0 - distance) * (2.0 - distance) * (1.0 - distance),
    )


def axis_weights(base, fraction, cells):
    local = fraction.shape[1]
    nodes = [
        spline_weight(fraction + 1.0),
        spline_weight(fraction),
        spline_weight(1.0 - fraction),
        spline_weight(2.0 - fraction),
    ]
    ids = lax.broadcasted_iota(jnp.int32, (cells, local), 0)
    total = jnp.zeros((cells, local), f32)
    for node in range(4):
        total = total + jnp.where(((base + (node - 1)) & (cells - 1)) == ids, nodes[node], 0.0)
    return total


def deposit_kernel(
    n, ok_ref, og_ref, pos_ref, str_ref, dye_ref, frac_ref, code_ref, vel_ref, grid_ref,
    part_ref, got_ref, send_sems, recv_sems,
):
    me = lax.axis_index("dom")
    barrier = pltpu.get_barrier_semaphore()
    for step in range(1, n):
        pl.semaphore_signal(barrier, inc=1, device_id={"dom": lax.rem(me + step, n)}, device_id_type=MESH)

    points = [pos_ref[i : i + 1, :] for i in range(3)]
    vortex = [str_ref[i : i + 1, :] for i in range(3)]
    first = [ok_ref[i : i + 1, :] + ok_ref[6 + i : 7 + i, :] for i in range(6)]
    second = [og_ref[i : i + 1, :] + og_ref[24 + i : 25 + i, :] for i in range(24)]
    turned = cross_rows(first[0:3], points)
    velocity = [turned[i] - first[3 + i] for i in range(3)]
    for i in range(3):
        vel_ref[i : i + 1, :] = velocity[i]
    term_one = cross_rows(first[0:3], vortex)
    dot_self = vortex[0] * points[0] + vortex[1] * points[1] + vortex[2] * points[2]
    mixed_one = [sum(vortex[k] * second[6 + 3 * k + i] for k in range(3)) for i in range(3)]
    mixed_two = [sum(vortex[k] * second[15 + 3 * k + i] for k in range(3)) for i in range(3)]
    slope_turned = cross_rows(second[0:3], points)
    mixed_turned = cross_rows(mixed_one, points)
    values = []
    for i in range(3):
        term_two = dot_self * (slope_turned[i] - second[3 + i]) - mixed_turned[i] + mixed_two[i]
        values.append((vortex[i] + 0.02 * (term_one[i] + term_two)) * 32.0)
    values.append(dye_ref[...] * 32.0)

    cell = code_ref[0:1, :]
    starts = [cell & 7, (cell >> 3) & 3, cell >> 5]
    weights = []
    for i in range(3):
        coords = starts[i].astype(f32) + frac_ref[i : i + 1, :] + 2.0 * velocity[i]
        lowest = jnp.floor(coords)
        weights.append(axis_weights(lowest.astype(jnp.int32), coords - lowest, 8 if i == 0 else 4))
    plane = [weights[2][z : z + 1, :] * weights[1][y : y + 1, :] for z in range(4) for y in range(4)]

    tile = code_ref[1:2, :]
    local = tile.shape[1]
    tiles = grid_ref.shape[0]
    ids = lax.broadcasted_iota(jnp.int32, (n * tiles, local), 0)
    onehot = jnp.where(ids == tile, 1.0, 0.0).astype(bf16)
    for c in range(4):
        spread = jnp.concatenate([weights[0] * (plane[k] * values[c]) for k in range(16)], 0)
        total = jnp.zeros((n * tiles, 128), f32)
        for piece in split(spread, 2):
            total = total + lax.dot_general(
                onehot, piece, (((1,), (1,)), ((), ())), preferred_element_type=f32
            )
        part_ref[:, :, c, :] = total.reshape(n, tiles, 128)

    pl.semaphore_wait(barrier, n - 1)
    copies = []
    for step in range(1, n):
        peer = lax.rem(me + step, n)
        copy = pltpu.make_async_remote_copy(
            src_ref=part_ref.at[peer],
            dst_ref=got_ref.at[step],
            send_sem=send_sems.at[step],
            recv_sem=recv_sems.at[step],
            device_id={"dom": peer},
            device_id_type=MESH,
        )
        copy.start()
        copies.append(copy)
    total = part_ref[me]
    for step in range(1, n):
        copies[step - 1].wait_recv()
        total = total + got_ref[step]
    grid_ref[...] = total
    for copy in copies:
        copy.wait_send()


def deposit(n, ok, og, positions, strength, dye, fraction, codes):
    local = positions.shape[1]
    tiles = local // 128
    return pl.pallas_call(
        functools.partial(deposit_kernel, n),
        out_shape=(
            jax.ShapeDtypeStruct((3, local), f32),
            jax.ShapeDtypeStruct((tiles, 4, 128), f32),
        ),
        in_specs=[pl.BlockSpec(memory_space=pltpu.VMEM)] * 7,
        out_specs=(pl.BlockSpec(memory_space=pltpu.VMEM),) * 2,
        scratch_shapes=[
            pltpu.VMEM((n, tiles, 4, 128), f32),
            pltpu.VMEM((n, tiles, 4, 128), f32),
            pltpu.SemaphoreType.DMA((n,)),
            pltpu.SemaphoreType.DMA((n,)),
        ],
        compiler_params=pltpu.CompilerParams(collective_id=1, has_side_effects=True, vmem_limit_bytes=48 << 20),
    )(ok, og, positions, strength, dye, fraction, codes)


def source_tables(blocks):
    points = [blocks[:, i].reshape(-1) for i in range(3)]
    vortex = [blocks[:, 3 + i].reshape(-1) for i in range(3)]
    radius = blocks[:, 6].reshape(-1)
    constant = points[0] * points[0] + points[1] * points[1] + points[2] * points[2] + radius * radius
    one = jnp.ones_like(radius).astype(bf16)
    rows = []
    for i in range(3):
        a, b, c = split_whole(-2.0 * points[i], 3)
        rows += [a, b, a, b, c, a, c, b]
    rows += split_whole(constant, 3) + [one] * 3 + [jnp.zeros_like(one)] * 2
    sources = jnp.stack(rows, axis=1)
    crossed = cross_rows(vortex, points)
    lead = [kernel_scale * v for v in vortex + crossed]
    slope = [-3.0 * v for v in lead]
    slope += [points[k] * slope[i] for k in range(3) for i in range(3)] + [
        points[k] * slope[3 + i] for k in range(3) for i in range(3)
    ]
    kernel_rows = jnp.stack(split_all(lead) + [jnp.zeros_like(one)] * 4)
    slope_rows = jnp.stack(split_all(slope))
    return sources, kernel_rows, slope_rows


def split_whole(value, parts):
    pieces = []
    for _ in range(parts):
        piece = lax.reduce_precision(value, 8, 7)
        pieces.append(piece.astype(bf16))
        value = value - piece
    return pieces


def split_all(rows):
    pairs = [split_whole(row, 2) for row in rows]
    return [pair[0] for pair in pairs] + [pair[1] for pair in pairs]


def target_table(positions):
    norm = positions[0] * positions[0] + positions[1] * positions[1] + positions[2] * positions[2]
    one = jnp.ones_like(norm).astype(bf16)
    rows = []
    for i in range(3):
        a, b, c = split_whole(positions[i], 3)
        rows += [a, a, b, b, a, c, b, c]
    rows += [one] * 3 + split_whole(norm, 3) + [jnp.zeros_like(one)] * 2
    return jnp.stack(rows)


def on_device(
    positions, strength, core_radius, dye_amount, cell_fraction, cell_index, tile_local, owner_dom
):
    n_dom, n_blk = lax.axis_size("dom"), lax.axis_size("blk")
    tiles = positions.shape[1] // 128
    block = jnp.concatenate([positions, strength, core_radius[None], core_radius[None]], axis=0)
    blocks = gather(block, n_blk)
    sources, kernel_rows, slope_rows = source_tables(blocks)
    ok, og = pair_sums(target_table(positions), sources, kernel_rows, slope_rows)
    codes = jnp.stack([cell_index, owner_dom[:, 0] * tiles + tile_local])
    return deposit(n_dom, ok, og, positions, strength, dye_amount[None], cell_fraction, codes)


def solution(mesh):
    both = ("dom", "blk")
    placed = (P(None, both), P(None, both), P(both), P(both), P(None, both), P(both), P(both), P(both, None))
    return jax.shard_map(
        on_device,
        mesh=mesh,
        in_specs=placed,
        out_specs=(P(None, both), P(both, None, None)),
        check_vma=False,
    )
```

```python
import functools
import math

import jax
import jax.numpy as jnp
from jax import lax
from jax.experimental import pallas as pl
from jax.experimental.pallas import tpu as pltpu
from jax.sharding import PartitionSpec as P

MESH = pl.DeviceIdType.MESH
f32, bf16 = jnp.float32, jnp.bfloat16
kernel_scale = 1.0 / (4.0 * math.pi)


def cross_rows(u, v):
    return [u[1] * v[2] - u[2] * v[1], u[2] * v[0] - u[0] * v[2], u[0] * v[1] - u[1] * v[0]]


def split(value, parts):
    pieces = []
    for _ in range(parts):
        piece = value.astype(bf16)
        pieces.append(piece)
        value = value - piece.astype(f32)
    return pieces


def spline_weight(distance):
    return jnp.where(
        distance < 1.0,
        1.0 - 2.5 * distance * distance + 1.5 * distance * distance * distance,
        0.5 * (2.0 - distance) * (2.0 - distance) * (1.0 - distance),
    )


def axis_weights(base, fraction, cells):
    local = fraction.shape[1]
    nodes = [
        spline_weight(fraction + 1.0),
        spline_weight(fraction),
        spline_weight(1.0 - fraction),
        spline_weight(2.0 - fraction),
    ]
    ids = lax.broadcasted_iota(jnp.int32, (cells, local), 0)
    total = jnp.zeros((cells, local), f32)
    for node in range(4):
        total = total + jnp.where(((base + (node - 1)) & (cells - 1)) == ids, nodes[node], 0.0)
    return total


TT, ST, CH = 256, 512, 64


def stack_split(value, parts):
    return [piece.astype(f32) for piece in split(value, parts)]


def step_kernel(
    n_dom, n_blk, pos_ref, str_ref, rad_ref, dye_ref, frac_ref, cell_ref, tile_ref, owner_ref,
    vel_ref, grid_ref,
    blocks_ref, tgt_ref, src_ref, rk_ref, rg_ref, ok_ref, og_ref, vk0, vk1, vg0, vg1, part_ref, got_ref,
    blk_send, blk_recv, dom_send, dom_recv,
):
    local = pos_ref.shape[1]
    dom, blk = lax.axis_index("dom"), lax.axis_index("blk")
    barrier = pltpu.get_barrier_semaphore()
    for step in range(1, n_blk):
        pl.semaphore_signal(barrier, inc=1, device_id={"blk": lax.rem(blk + step, n_blk)}, device_id_type=MESH)
    for step in range(1, n_dom):
        pl.semaphore_signal(barrier, inc=1, device_id={"dom": lax.rem(dom + step, n_dom)}, device_id_type=MESH)

    points = [pos_ref[i : i + 1, :] for i in range(3)]
    vortex = [str_ref[i : i + 1, :] for i in range(3)]
    radius = rad_ref[...]
    norm = points[0] * points[0] + points[1] * points[1] + points[2] * points[2]
    one, zero = jnp.ones_like(norm), jnp.zeros_like(norm)
    lead = [kernel_scale * row for row in vortex + cross_rows(vortex, points)]
    blocks_ref[0, 0:8, :] = jnp.concatenate(lead + [zero] * 2, 0)
    blocks_ref[0, 8:16, :] = jnp.concatenate(
        [-2.0 * row for row in points] + [norm + radius * radius, one] + [zero] * 3, 0
    )
    pl.semaphore_wait(barrier, n_blk - 1 + n_dom - 1)

    steps = list(range(2, n_blk, 2)) + list(range(1, n_blk, 2))
    blk_copies = []
    for slot, step in enumerate(steps, 1):
        copy = pltpu.make_async_remote_copy(
            src_ref=blocks_ref.at[0],
            dst_ref=blocks_ref.at[slot],
            send_sem=blk_send.at[slot],
            recv_sem=blk_recv.at[slot],
            device_id={"blk": lax.rem(blk + step, n_blk)},
            device_id_type=MESH,
        )
        copy.start()
        blk_copies.append(copy)

    t1, t2, t3 = stack_split(jnp.concatenate(points + [one, norm] + [zero] * 3, 0), 3)
    tgt_ref[...] = jnp.concatenate([t1, t2, t3, t1, t2, t1], 0).astype(bf16)
    ok_ref[...] = jnp.zeros_like(ok_ref)
    og_ref[...] = jnp.zeros_like(og_ref)

    vk, vg = (vk0, vk1), (vg0, vg1)
    chunks = local // ST
    count = chunks * (local // TT)

    def values(index, slot):
        start = pl.multiple_of(lax.rem(index, chunks) * ST, ST)
        targets = tgt_ref[:, pl.ds(pl.multiple_of(index // chunks * TT, TT), TT)]
        for row in range(0, ST, CH):
            square = jnp.dot(
                src_ref[pl.ds(pl.multiple_of(start + row, CH), CH), :], targets, preferred_element_type=f32
            )
            inverse = lax.rsqrt(square)
            second = inverse * inverse
            kern = second * inverse
            slope = kern * second
            kern_hi = kern.astype(bf16)
            slope_hi = slope.astype(bf16)
            vk[slot][row : row + CH, :] = kern_hi
            vg[slot][row : row + CH, :] = slope_hi
            vk[slot][ST + row : ST + row + CH, :] = (kern - kern_hi.astype(f32)).astype(bf16)
            vg[slot][ST + row : ST + row + CH, :] = (slope - slope_hi.astype(f32)).astype(bf16)

    def sums(index, slot):
        start = pl.multiple_of(lax.rem(index, chunks) * ST, ST)
        at = pl.multiple_of(index // chunks * TT, TT)
        rk = rk_ref[:, pl.ds(start, ST)]
        rg = rg_ref[:, pl.ds(start, ST)]
        ok_ref[:, pl.ds(at, TT)] += jnp.dot(
            jnp.concatenate([rk, rk], 1), vk[slot][...], preferred_element_type=f32
        )
        og_ref[:, pl.ds(at, TT)] += jnp.dot(
            jnp.concatenate([rg, rg], 1), vg[slot][...], preferred_element_type=f32
        )

    def block_tables(block):
        lead = blocks_ref[block, 0:8, :]
        place = blocks_ref[block, 8:16, :]
        hi, lo = split(lead, 2)
        rk_ref[0:8, :] = hi
        rk_ref[8:16, :] = lo
        for k in range(4):
            rows = lead if k == 0 else place[k - 1 : k, :] * lead
            hi, lo = split(rows, 2)
            rg_ref[8 * k : 8 * k + 8, :] = hi
            rg_ref[32 + 8 * k : 40 + 8 * k, :] = lo
        for at in range(0, local, 128):
            s1, s2, s3 = stack_split(place[:, at : at + 128], 3)
            src_ref[at : at + 128, :] = jnp.concatenate([s1, s1, s1, s2, s2, s3], 0).T.astype(bf16)

    @pl.loop(0, n_blk)
    def _(block):
        @pl.when(block > 0)
        def _():
            pltpu.make_async_remote_copy(
                src_ref=blocks_ref.at[0],
                dst_ref=blocks_ref.at[block],
                send_sem=blk_send.at[block],
                recv_sem=blk_recv.at[block],
                device_id={"blk": lax.rem(blk + 1, n_blk)},
                device_id_type=MESH,
            ).wait_recv()

        block_tables(block)
        values(0, 0)

        @pl.loop(0, count // 2)
        def _(pair):
            values(2 * pair + 1, 1)
            sums(2 * pair, 0)
            values(jnp.minimum(2 * pair + 2, count - 1), 0)
            sums(2 * pair + 1, 1)

    for copy in blk_copies:
        copy.wait_send()

    first = ok_ref[0:8, :] + ok_ref[8:16, :]
    first = [first[i : i + 1, :] for i in range(6)]
    second = []
    for k in range(4):
        rows = og_ref[8 * k : 8 * k + 8, :] + og_ref[32 + 8 * k : 40 + 8 * k, :]
        second.append([rows[i : i + 1, :] for i in range(6)])
    turned = cross_rows(first[0:3], points)
    velocity = [turned[i] - first[3 + i] for i in range(3)]
    for i in range(3):
        vel_ref[i : i + 1, :] = velocity[i]
    term_one = cross_rows(first[0:3], vortex)
    dot_self = vortex[0] * points[0] + vortex[1] * points[1] + vortex[2] * points[2]
    mixed_one = [-0.5 * sum(vortex[k] * second[1 + k][i] for k in range(3)) for i in range(3)]
    mixed_two = [-0.5 * sum(vortex[k] * second[1 + k][3 + i] for k in range(3)) for i in range(3)]
    slope_turned = cross_rows(second[0][0:3], points)
    mixed_turned = cross_rows(mixed_one, points)
    carried = []
    for i in range(3):
        term_two = dot_self * (slope_turned[i] - second[0][3 + i]) - mixed_turned[i] + mixed_two[i]
        carried.append((vortex[i] + 0.02 * (term_one[i] - 3.0 * term_two)) * 32.0)
    carried.append(dye_ref[...] * 32.0)

    cell = cell_ref[...]
    starts = [cell & 7, (cell >> 3) & 3, cell >> 5]
    weights = []
    for i in range(3):
        coords = starts[i].astype(f32) + frac_ref[i : i + 1, :] + 2.0 * velocity[i]
        lowest = jnp.floor(coords)
        weights.append(axis_weights(lowest.astype(jnp.int32), coords - lowest, 8 if i == 0 else 4))
    plane = [weights[2][z : z + 1, :] * weights[1][y : y + 1, :] for z in range(4) for y in range(4)]

    tiles = grid_ref.shape[0]
    tile = owner_ref[...] * tiles + tile_ref[...]
    ids = lax.broadcasted_iota(jnp.int32, (n_dom * tiles, local), 0)
    onehot = jnp.where(ids == tile, 1.0, 0.0).astype(bf16)
    for c in range(4):
        spread = jnp.concatenate([weights[0] * (plane[k] * carried[c]) for k in range(16)], 0)
        total = jnp.zeros((n_dom * tiles, 128), f32)
        for piece in split(spread, 2):
            total = total + lax.dot_general(
                onehot, piece, (((1,), (1,)), ((), ())), preferred_element_type=f32
            )
        part_ref[:, :, c, :] = total.reshape(n_dom, tiles, 128)

    dom_copies = []
    for step in range(1, n_dom):
        peer = lax.rem(dom + step, n_dom)
        copy = pltpu.make_async_remote_copy(
            src_ref=part_ref.at[peer],
            dst_ref=got_ref.at[step],
            send_sem=dom_send.at[step],
            recv_sem=dom_recv.at[step],
            device_id={"dom": peer},
            device_id_type=MESH,
        )
        copy.start()
        dom_copies.append(copy)
    total = part_ref[dom]
    for step in range(1, n_dom):
        dom_copies[step - 1].wait_recv()
        total = total + got_ref[step]
    grid_ref[...] = total
    for copy in dom_copies:
        copy.wait_send()


def on_device(
    positions, strength, core_radius, dye_amount, cell_fraction, cell_index, tile_local, owner_dom
):
    n_dom, n_blk = lax.axis_size("dom"), lax.axis_size("blk")
    local = positions.shape[1]
    tiles = local // 128
    vmem = pl.BlockSpec(memory_space=pltpu.VMEM)
    return pl.pallas_call(
        functools.partial(step_kernel, n_dom, n_blk),
        out_shape=(
            jax.ShapeDtypeStruct((3, local), f32),
            jax.ShapeDtypeStruct((tiles, 4, 128), f32),
        ),
        in_specs=[vmem] * 8,
        out_specs=(vmem, vmem),
        scratch_shapes=[
            pltpu.VMEM((n_blk, 16, local), f32),
            pltpu.VMEM((48, local), bf16),
            pltpu.VMEM((local, 48), bf16),
            pltpu.VMEM((16, local), bf16),
            pltpu.VMEM((64, local), bf16),
            pltpu.VMEM((16, local), f32),
            pltpu.VMEM((64, local), f32),
        ]
        + [pltpu.VMEM((2 * ST, TT), bf16)] * 4
        + [pltpu.VMEM((n_dom, tiles, 4, 128), f32)] * 2
        + [pltpu.SemaphoreType.DMA((n_blk,))] * 2
        + [pltpu.SemaphoreType.DMA((n_dom,))] * 2,
        compiler_params=pltpu.CompilerParams(collective_id=0, has_side_effects=True, vmem_limit_bytes=56 << 20),
    )(
        positions, strength, core_radius[None], dye_amount[None], cell_fraction, cell_index[None],
        tile_local[None], owner_dom.reshape(1, local),
    )


def solution(mesh):
    both = ("dom", "blk")
    placed = (P(None, both), P(None, both), P(both), P(both), P(None, both), P(both), P(both), P(both, None))
    return jax.shard_map(
        on_device,
        mesh=mesh,
        in_specs=placed,
        out_specs=(P(None, both), P(both, None, None)),
        check_vma=False,
    )
```

```python
import functools
import math

import jax
import jax.numpy as jnp
from jax import lax
from jax.experimental import pallas as pl
from jax.experimental.pallas import tpu as pltpu
from jax.sharding import PartitionSpec as P

MESH = pl.DeviceIdType.MESH
f32, bf16 = jnp.float32, jnp.bfloat16
kernel_scale = 1.0 / (4.0 * math.pi)


def cross_rows(u, v):
    return [u[1] * v[2] - u[2] * v[1], u[2] * v[0] - u[0] * v[2], u[0] * v[1] - u[1] * v[0]]


def split(value, parts):
    pieces = []
    for _ in range(parts):
        piece = value.astype(bf16)
        pieces.append(piece)
        value = value - piece.astype(f32)
    return pieces


def spline_weight(distance):
    return jnp.where(
        distance < 1.0,
        1.0 - 2.5 * distance * distance + 1.5 * distance * distance * distance,
        0.5 * (2.0 - distance) * (2.0 - distance) * (1.0 - distance),
    )


def axis_weights(base, fraction, cells):
    local = fraction.shape[1]
    nodes = [
        spline_weight(fraction + 1.0),
        spline_weight(fraction),
        spline_weight(1.0 - fraction),
        spline_weight(2.0 - fraction),
    ]
    ids = lax.broadcasted_iota(jnp.int32, (cells, local), 0)
    total = jnp.zeros((cells, local), f32)
    for node in range(4):
        total = total + jnp.where(((base + (node - 1)) & (cells - 1)) == ids, nodes[node], 0.0)
    return total


TT, ST, UNROLL = 256, 512, 16


def stack_split(value, parts):
    return [piece.astype(f32) for piece in split(value, parts)]


def step_kernel(
    n_dom, n_blk, pos_ref, str_ref, rad_ref, dye_ref, frac_ref, cell_ref, tile_ref, owner_ref,
    vel_ref, grid_ref,
    blocks_ref, tgt_ref, src_ref, rk_ref, rg_ref, ok_ref, og_ref, q0, q1, vk0, vk1, vg0, vg1, part_ref, got_ref,
    blk_send, blk_recv, dom_send, dom_recv,
):
    local = pos_ref.shape[1]
    dom, blk = lax.axis_index("dom"), lax.axis_index("blk")
    barrier = pltpu.get_barrier_semaphore()
    for step in range(1, n_blk):
        pl.semaphore_signal(barrier, inc=1, device_id={"blk": lax.rem(blk + step, n_blk)}, device_id_type=MESH)
    for step in range(1, n_dom):
        pl.semaphore_signal(barrier, inc=1, device_id={"dom": lax.rem(dom + step, n_dom)}, device_id_type=MESH)

    points = [pos_ref[i : i + 1, :] for i in range(3)]
    vortex = [str_ref[i : i + 1, :] for i in range(3)]
    radius = rad_ref[...]
    norm = points[0] * points[0] + points[1] * points[1] + points[2] * points[2]
    one, zero = jnp.ones_like(norm), jnp.zeros_like(norm)
    lead = [kernel_scale * row for row in vortex + cross_rows(vortex, points)]
    blocks_ref[0, 0:8, :] = jnp.concatenate(lead + [zero] * 2, 0)
    blocks_ref[0, 8:16, :] = jnp.concatenate(
        [-2.0 * row for row in points] + [norm + radius * radius, one] + [zero] * 3, 0
    )
    pl.semaphore_wait(barrier, n_blk - 1 + n_dom - 1)

    steps = list(range(2, n_blk, 2)) + list(range(1, n_blk, 2))
    blk_copies = []
    for slot, step in enumerate(steps, 1):
        copy = pltpu.make_async_remote_copy(
            src_ref=blocks_ref.at[0],
            dst_ref=blocks_ref.at[slot],
            send_sem=blk_send.at[slot],
            recv_sem=blk_recv.at[slot],
            device_id={"blk": lax.rem(blk + step, n_blk)},
            device_id_type=MESH,
        )
        copy.start()
        blk_copies.append(copy)

    t1, t2, t3 = stack_split(jnp.concatenate(points + [one, norm] + [zero] * 3, 0), 3)
    tgt_ref[...] = jnp.concatenate([t1, t2, t3, t1, t2, t1], 0).astype(bf16)
    ok_ref[...] = jnp.zeros_like(ok_ref)
    og_ref[...] = jnp.zeros_like(og_ref)

    qs, vk, vg = (q0, q1), (vk0, vk1), (vg0, vg1)
    chunks = local // ST
    count = chunks * (local // TT)
    halves = count // UNROLL

    def place_of(index):
        step = lax.rem(index, count)
        return (
            lax.rem(index // count, 2),
            pl.multiple_of(lax.rem(step, chunks) * ST, ST),
            pl.multiple_of(step // chunks * TT, TT),
        )

    def squares(index, slot):
        side, start, at = place_of(index)
        qs[slot][...] = jnp.dot(
            src_ref[side, pl.ds(start, ST), :], tgt_ref[:, pl.ds(at, TT)], preferred_element_type=f32
        )

    def values(slot):
        inverse = lax.rsqrt(qs[slot][...])
        second = inverse * inverse
        kern = second * inverse
        slope = kern * second
        kern_hi = kern.astype(bf16)
        slope_hi = slope.astype(bf16)
        vk[slot][0:ST, :] = kern_hi
        vg[slot][0:ST, :] = slope_hi
        vk[slot][ST:, :] = (kern - kern_hi.astype(f32)).astype(bf16)
        vg[slot][ST:, :] = (slope - slope_hi.astype(f32)).astype(bf16)

    def sums(index, slot):
        side, start, at = place_of(index)
        rk = rk_ref[side, :, pl.ds(start, ST)]
        rg = rg_ref[side, :, pl.ds(start, ST)]
        ok_ref[:, pl.ds(at, TT)] += jnp.dot(
            jnp.concatenate([rk, rk], 1), vk[slot][...], preferred_element_type=f32
        )
        og_ref[:, pl.ds(at, TT)] += jnp.dot(
            jnp.concatenate([rg, rg], 1), vg[slot][...], preferred_element_type=f32
        )

    def block_tables(block):
        side = lax.rem(block, 2)
        lead = blocks_ref[block, 0:8, :]
        place = blocks_ref[block, 8:16, :]
        hi, lo = split(lead, 2)
        rk_ref[side, 0:8, :] = hi
        rk_ref[side, 8:16, :] = lo
        for k in range(4):
            rows = lead if k == 0 else place[k - 1 : k, :] * lead
            hi, lo = split(rows, 2)
            rg_ref[side, 8 * k : 8 * k + 8, :] = hi
            rg_ref[side, 32 + 8 * k : 40 + 8 * k, :] = lo
        for at in range(0, local, 128):
            s1, s2, s3 = stack_split(place[:, at : at + 128], 3)
            src_ref[side, at : at + 128, :] = jnp.concatenate([s1, s1, s1, s2, s2, s3], 0).T.astype(bf16)

    block_tables(0)
    squares(0, 0)
    values(0)
    squares(1, 1)

    @pl.loop(0, n_blk * halves)
    def _(part):
        block = part // halves + 1

        @pl.when((lax.rem(part, halves) == halves - 1) & (block < n_blk))
        def _():
            pltpu.make_async_remote_copy(
                src_ref=blocks_ref.at[0],
                dst_ref=blocks_ref.at[block],
                send_sem=blk_send.at[block],
                recv_sem=blk_recv.at[block],
                device_id={"blk": lax.rem(blk + 1, n_blk)},
                device_id_type=MESH,
            ).wait_recv()
            block_tables(block)

        for step in range(UNROLL):
            index = UNROLL * part + step
            slot = step % 2
            sums(index, slot)
            values(1 - slot)
            squares(jnp.minimum(index + 2, n_blk * count - 1), slot)

    for copy in blk_copies:
        copy.wait_send()

    first = ok_ref[0:8, :] + ok_ref[8:16, :]
    first = [first[i : i + 1, :] for i in range(6)]
    second = []
    for k in range(4):
        rows = og_ref[8 * k : 8 * k + 8, :] + og_ref[32 + 8 * k : 40 + 8 * k, :]
        second.append([rows[i : i + 1, :] for i in range(6)])
    turned = cross_rows(first[0:3], points)
    velocity = [turned[i] - first[3 + i] for i in range(3)]
    for i in range(3):
        vel_ref[i : i + 1, :] = velocity[i]
    term_one = cross_rows(first[0:3], vortex)
    dot_self = vortex[0] * points[0] + vortex[1] * points[1] + vortex[2] * points[2]
    mixed_one = [-0.5 * sum(vortex[k] * second[1 + k][i] for k in range(3)) for i in range(3)]
    mixed_two = [-0.5 * sum(vortex[k] * second[1 + k][3 + i] for k in range(3)) for i in range(3)]
    slope_turned = cross_rows(second[0][0:3], points)
    mixed_turned = cross_rows(mixed_one, points)
    carried = []
    for i in range(3):
        term_two = dot_self * (slope_turned[i] - second[0][3 + i]) - mixed_turned[i] + mixed_two[i]
        carried.append((vortex[i] + 0.02 * (term_one[i] - 3.0 * term_two)) * 32.0)
    carried.append(dye_ref[...] * 32.0)

    cell = cell_ref[...]
    starts = [cell & 7, (cell >> 3) & 3, cell >> 5]
    weights = []
    for i in range(3):
        coords = starts[i].astype(f32) + frac_ref[i : i + 1, :] + 2.0 * velocity[i]
        lowest = jnp.floor(coords)
        weights.append(axis_weights(lowest.astype(jnp.int32), coords - lowest, 8 if i == 0 else 4))
    plane = [weights[2][z : z + 1, :] * weights[1][y : y + 1, :] for z in range(4) for y in range(4)]

    tiles = grid_ref.shape[0]
    tile = owner_ref[...] * tiles + tile_ref[...]
    ids = lax.broadcasted_iota(jnp.int32, (n_dom * tiles, local), 0)
    onehot = jnp.where(ids == tile, 1.0, 0.0).astype(bf16)
    for c in range(4):
        spread = jnp.concatenate([weights[0] * (plane[k] * carried[c]) for k in range(16)], 0)
        total = jnp.zeros((n_dom * tiles, 128), f32)
        for piece in split(spread, 2):
            total = total + lax.dot_general(
                onehot, piece, (((1,), (1,)), ((), ())), preferred_element_type=f32
            )
        part_ref[:, :, c, :] = total.reshape(n_dom, tiles, 128)

    dom_copies = []
    for step in range(1, n_dom):
        peer = lax.rem(dom + step, n_dom)
        copy = pltpu.make_async_remote_copy(
            src_ref=part_ref.at[peer],
            dst_ref=got_ref.at[step],
            send_sem=dom_send.at[step],
            recv_sem=dom_recv.at[step],
            device_id={"dom": peer},
            device_id_type=MESH,
        )
        copy.start()
        dom_copies.append(copy)
    total = part_ref[dom]
    for step in range(1, n_dom):
        dom_copies[step - 1].wait_recv()
        total = total + got_ref[step]
    grid_ref[...] = total
    for copy in dom_copies:
        copy.wait_send()


def on_device(
    positions, strength, core_radius, dye_amount, cell_fraction, cell_index, tile_local, owner_dom
):
    n_dom, n_blk = lax.axis_size("dom"), lax.axis_size("blk")
    local = positions.shape[1]
    tiles = local // 128
    vmem = pl.BlockSpec(memory_space=pltpu.VMEM)
    return pl.pallas_call(
        functools.partial(step_kernel, n_dom, n_blk),
        out_shape=(
            jax.ShapeDtypeStruct((3, local), f32),
            jax.ShapeDtypeStruct((tiles, 4, 128), f32),
        ),
        in_specs=[vmem] * 8,
        out_specs=(vmem, vmem),
        scratch_shapes=[
            pltpu.VMEM((n_blk, 16, local), f32),
            pltpu.VMEM((48, local), bf16),
            pltpu.VMEM((2, local, 48), bf16),
            pltpu.VMEM((2, 16, local), bf16),
            pltpu.VMEM((2, 64, local), bf16),
            pltpu.VMEM((16, local), f32),
            pltpu.VMEM((64, local), f32),
        ]
        + [pltpu.VMEM((ST, TT), f32)] * 2
        + [pltpu.VMEM((2 * ST, TT), bf16)] * 4
        + [pltpu.VMEM((n_dom, tiles, 4, 128), f32)] * 2
        + [pltpu.SemaphoreType.DMA((n_blk,))] * 2
        + [pltpu.SemaphoreType.DMA((n_dom,))] * 2,
        compiler_params=pltpu.CompilerParams(collective_id=0, has_side_effects=True, vmem_limit_bytes=56 << 20),
    )(
        positions, strength, core_radius[None], dye_amount[None], cell_fraction, cell_index[None],
        tile_local[None], owner_dom.reshape(1, local),
    )


def solution(mesh):
    both = ("dom", "blk")
    placed = (P(None, both), P(None, both), P(both), P(both), P(None, both), P(both), P(both), P(both, None))
    return jax.shard_map(
        on_device,
        mesh=mesh,
        in_specs=placed,
        out_specs=(P(None, both), P(both, None, None)),
        check_vma=False,
    )
```

```python
import functools
import math

import jax
import jax.numpy as jnp
from jax import lax
from jax.experimental import pallas as pl
from jax.experimental.pallas import tpu as pltpu
from jax.sharding import PartitionSpec as P

MESH = pl.DeviceIdType.MESH
f32, bf16 = jnp.float32, jnp.bfloat16
kernel_scale = 1.0 / (4.0 * math.pi)


def cross_rows(u, v):
    return [u[1] * v[2] - u[2] * v[1], u[2] * v[0] - u[0] * v[2], u[0] * v[1] - u[1] * v[0]]


def split(value, parts):
    pieces = []
    for _ in range(parts):
        piece = value.astype(bf16)
        pieces.append(piece)
        value = value - piece.astype(f32)
    return pieces


def spline_weight(distance):
    return jnp.where(
        distance < 1.0,
        1.0 - 2.5 * distance * distance + 1.5 * distance * distance * distance,
        0.5 * (2.0 - distance) * (2.0 - distance) * (1.0 - distance),
    )


def axis_weights(base, fraction, cells):
    local = fraction.shape[1]
    nodes = [
        spline_weight(fraction + 1.0),
        spline_weight(fraction),
        spline_weight(1.0 - fraction),
        spline_weight(2.0 - fraction),
    ]
    ids = lax.broadcasted_iota(jnp.int32, (cells, local), 0)
    total = jnp.zeros((cells, local), f32)
    for node in range(4):
        total = total + jnp.where(((base + (node - 1)) & (cells - 1)) == ids, nodes[node], 0.0)
    return total


TT, ST, PIECE, CHUNK, UNROLL = 256, 512, 128, 32, 16


def stack_split(value, parts):
    return [piece.astype(f32) for piece in split(value, parts)]


def step_kernel(
    n_dom, n_blk, pos_ref, str_ref, rad_ref, dye_ref, frac_ref, cell_ref, tile_ref, owner_ref,
    vel_ref, grid_ref,
    blocks_ref, tgt_ref, src_ref, rk_ref, rg_ref, ok_ref, og_ref, q0, q1, part_ref, got_ref,
    blk_send, blk_recv, dom_send, dom_recv,
):
    local = pos_ref.shape[1]
    dom, blk = lax.axis_index("dom"), lax.axis_index("blk")
    barrier = pltpu.get_barrier_semaphore()
    for step in range(1, n_blk):
        pl.semaphore_signal(barrier, inc=1, device_id={"blk": lax.rem(blk + step, n_blk)}, device_id_type=MESH)
    for step in range(1, n_dom):
        pl.semaphore_signal(barrier, inc=1, device_id={"dom": lax.rem(dom + step, n_dom)}, device_id_type=MESH)

    points = [pos_ref[i : i + 1, :] for i in range(3)]
    vortex = [str_ref[i : i + 1, :] for i in range(3)]
    radius = rad_ref[...]
    norm = points[0] * points[0] + points[1] * points[1] + points[2] * points[2]
    one, zero = jnp.ones_like(norm), jnp.zeros_like(norm)
    lead = [kernel_scale * row for row in vortex + cross_rows(vortex, points)]
    blocks_ref[0, 0:8, :] = jnp.concatenate(lead + [zero] * 2, 0)
    blocks_ref[0, 8:16, :] = jnp.concatenate(
        [-2.0 * row for row in points] + [norm + radius * radius, one] + [zero] * 3, 0
    )
    pl.semaphore_wait(barrier, n_blk - 1 + n_dom - 1)

    steps = list(range(2, n_blk, 2)) + list(range(1, n_blk, 2))
    blk_copies = []
    for slot, step in enumerate(steps, 1):
        copy = pltpu.make_async_remote_copy(
            src_ref=blocks_ref.at[0],
            dst_ref=blocks_ref.at[slot],
            send_sem=blk_send.at[slot],
            recv_sem=blk_recv.at[slot],
            device_id={"blk": lax.rem(blk + step, n_blk)},
            device_id_type=MESH,
        )
        copy.start()
        blk_copies.append(copy)

    t1, t2, t3 = stack_split(jnp.concatenate(points + [one, norm] + [zero] * 3, 0), 3)
    tgt_ref[...] = jnp.concatenate([t1, t2, t3, t1, t2, t1], 0).astype(bf16)
    ok_ref[...] = jnp.zeros_like(ok_ref)
    og_ref[...] = jnp.zeros_like(og_ref)

    qs = (q0, q1)
    chunks = local // ST
    count = chunks * (local // TT)
    halves = count // UNROLL

    def place_of(index):
        step = lax.rem(index, count)
        return (
            lax.rem(index // count, 2),
            pl.multiple_of(lax.rem(step, chunks) * ST, ST),
            pl.multiple_of(step // chunks * TT, TT),
        )

    def squares(index, slot, row):
        side, start, at = place_of(index)
        qs[slot][row : row + PIECE, :] = jnp.dot(
            src_ref[side, pl.ds(pl.multiple_of(start + row, PIECE), PIECE), :],
            tgt_ref[:, pl.ds(at, TT)],
            preferred_element_type=f32,
        )

    def values(slot, row, kern_parts, slope_parts):
        for at in range(row, row + PIECE, CHUNK):
            inverse = lax.rsqrt(qs[slot][at : at + CHUNK, :])
            second = inverse * inverse
            kern = second * inverse
            slope = kern * second
            kern_hi = kern.astype(bf16)
            slope_hi = slope.astype(bf16)
            kern_parts += [kern_hi, (kern - kern_hi.astype(f32)).astype(bf16)]
            slope_parts += [slope_hi, (slope - slope_hi.astype(f32)).astype(bf16)]

    def sums(index, kern_parts, slope_parts):
        side, start, at = place_of(index)
        twice = pl.ds(pl.multiple_of(2 * start, 2 * ST), 2 * ST)
        ok_ref[:, pl.ds(at, TT)] += jnp.dot(
            rk_ref[side, :, twice], jnp.concatenate(kern_parts, 0), preferred_element_type=f32
        )
        og_ref[:, pl.ds(at, TT)] += jnp.dot(
            rg_ref[side, :, twice], jnp.concatenate(slope_parts, 0), preferred_element_type=f32
        )

    column = lax.broadcasted_iota(jnp.int32, (128, 256), 1)
    origin = (column // (2 * CHUNK)) * CHUNK + column % CHUNK
    double = jnp.where(lax.broadcasted_iota(jnp.int32, (128, 256), 0) == origin, 1.0, 0.0).astype(bf16)

    def block_tables(block):
        side = lax.rem(block, 2)
        lead = blocks_ref[block, 0:8, :]
        place = blocks_ref[block, 8:16, :]
        groups = [split(lead if k == 0 else place[k - 1 : k, :] * lead, 2) for k in range(4)]
        rows = jnp.concatenate(
            [g.astype(f32) for g in groups[0]]
            + [g[0].astype(f32) for g in groups]
            + [g[1].astype(f32) for g in groups],
            0,
        ).astype(bf16)
        doubled = jnp.dot(
            jnp.concatenate([rows[:, at : at + 128] for at in range(0, local, 128)], 0),
            double,
            preferred_element_type=f32,
        ).astype(bf16)
        for k in range(local // 128):
            rk_ref[side, :, 256 * k : 256 * k + 256] = doubled[80 * k : 80 * k + 16]
            rg_ref[side, :, 256 * k : 256 * k + 256] = doubled[80 * k + 16 : 80 * k + 80]
        for at in range(0, local, 128):
            s1, s2, s3 = stack_split(place[:, at : at + 128], 3)
            src_ref[side, at : at + 128, :] = jnp.concatenate([s1, s1, s1, s2, s2, s3], 0).T.astype(bf16)

    block_tables(0)
    for row in range(0, ST, PIECE):
        squares(0, 0, row)

    @pl.loop(0, n_blk * halves)
    def _(part):
        block = part // halves + 1

        @pl.when((lax.rem(part, halves) == halves - 1) & (block < n_blk))
        def _():
            pltpu.make_async_remote_copy(
                src_ref=blocks_ref.at[0],
                dst_ref=blocks_ref.at[block],
                send_sem=blk_send.at[block],
                recv_sem=blk_recv.at[block],
                device_id={"blk": lax.rem(blk + 1, n_blk)},
                device_id_type=MESH,
            ).wait_recv()
            block_tables(block)

        for step in range(UNROLL):
            index = UNROLL * part + step
            slot = step % 2
            kern_parts, slope_parts = [], []
            for row in range(0, ST, PIECE):
                squares(jnp.minimum(index + 1, n_blk * count - 1), 1 - slot, row)
                values(slot, row, kern_parts, slope_parts)
            sums(index, kern_parts, slope_parts)

    for copy in blk_copies:
        copy.wait_send()

    first = ok_ref[0:8, :] + ok_ref[8:16, :]
    first = [first[i : i + 1, :] for i in range(6)]
    second = []
    for k in range(4):
        rows = og_ref[8 * k : 8 * k + 8, :] + og_ref[32 + 8 * k : 40 + 8 * k, :]
        second.append([rows[i : i + 1, :] for i in range(6)])
    turned = cross_rows(first[0:3], points)
    velocity = [turned[i] - first[3 + i] for i in range(3)]
    for i in range(3):
        vel_ref[i : i + 1, :] = velocity[i]
    term_one = cross_rows(first[0:3], vortex)
    dot_self = vortex[0] * points[0] + vortex[1] * points[1] + vortex[2] * points[2]
    mixed_one = [-0.5 * sum(vortex[k] * second[1 + k][i] for k in range(3)) for i in range(3)]
    mixed_two = [-0.5 * sum(vortex[k] * second[1 + k][3 + i] for k in range(3)) for i in range(3)]
    slope_turned = cross_rows(second[0][0:3], points)
    mixed_turned = cross_rows(mixed_one, points)
    carried = []
    for i in range(3):
        term_two = dot_self * (slope_turned[i] - second[0][3 + i]) - mixed_turned[i] + mixed_two[i]
        carried.append((vortex[i] + 0.02 * (term_one[i] - 3.0 * term_two)) * 32.0)
    carried.append(dye_ref[...] * 32.0)

    cell = cell_ref[...]
    starts = [cell & 7, (cell >> 3) & 3, cell >> 5]
    weights = []
    for i in range(3):
        coords = starts[i].astype(f32) + frac_ref[i : i + 1, :] + 2.0 * velocity[i]
        lowest = jnp.floor(coords)
        weights.append(axis_weights(lowest.astype(jnp.int32), coords - lowest, 8 if i == 0 else 4))
    plane = [weights[2][z : z + 1, :] * weights[1][y : y + 1, :] for z in range(4) for y in range(4)]

    tiles = grid_ref.shape[0]
    tile = owner_ref[...] * tiles + tile_ref[...]
    ids = lax.broadcasted_iota(jnp.int32, (n_dom * tiles, local), 0)
    onehot = jnp.where(ids == tile, 1.0, 0.0).astype(bf16)
    twice = jnp.concatenate([onehot, onehot], 1)
    dom_copies = []
    for pair in range(2):
        spread = jnp.concatenate(
            [weights[0] * (plane[k] * carried[2 * pair + c]) for c in range(2) for k in range(16)], 0
        )
        part_ref[pair] = lax.dot_general(
            twice,
            jnp.concatenate(split(spread, 2), 1),
            (((1,), (1,)), ((), ())),
            preferred_element_type=f32,
        ).reshape(n_dom, tiles, 256)
        for step in range(1, n_dom):
            peer = lax.rem(dom + step, n_dom)
            copy = pltpu.make_async_remote_copy(
                src_ref=part_ref.at[pair, peer],
                dst_ref=got_ref.at[pair, step],
                send_sem=dom_send.at[pair, step],
                recv_sem=dom_recv.at[pair, step],
                device_id={"dom": peer},
                device_id_type=MESH,
            )
            copy.start()
            dom_copies.append(copy)
    for pair in range(2):
        total = part_ref[pair, dom]
        for step in range(1, n_dom):
            dom_copies[pair * (n_dom - 1) + step - 1].wait_recv()
            total = total + got_ref[pair, step]
        for c in range(2):
            grid_ref[:, 2 * pair + c, :] = total[:, 128 * c : 128 * c + 128]
    for copy in dom_copies:
        copy.wait_send()


def on_device(
    positions, strength, core_radius, dye_amount, cell_fraction, cell_index, tile_local, owner_dom
):
    n_dom, n_blk = lax.axis_size("dom"), lax.axis_size("blk")
    local = positions.shape[1]
    tiles = local // 128
    vmem = pl.BlockSpec(memory_space=pltpu.VMEM)
    return pl.pallas_call(
        functools.partial(step_kernel, n_dom, n_blk),
        out_shape=(
            jax.ShapeDtypeStruct((3, local), f32),
            jax.ShapeDtypeStruct((tiles, 4, 128), f32),
        ),
        in_specs=[vmem] * 8,
        out_specs=(vmem, vmem),
        scratch_shapes=[
            pltpu.VMEM((n_blk, 16, local), f32),
            pltpu.VMEM((48, local), bf16),
            pltpu.VMEM((2, local, 48), bf16),
            pltpu.VMEM((2, 16, 2 * local), bf16),
            pltpu.VMEM((2, 64, 2 * local), bf16),
            pltpu.VMEM((16, local), f32),
            pltpu.VMEM((64, local), f32),
        ]
        + [pltpu.VMEM((ST, TT), f32)] * 2
        + [pltpu.VMEM((2, n_dom, tiles, 256), f32)] * 2
        + [pltpu.SemaphoreType.DMA((n_blk,))] * 2
        + [pltpu.SemaphoreType.DMA((2, n_dom))] * 2,
        compiler_params=pltpu.CompilerParams(collective_id=0, has_side_effects=True, vmem_limit_bytes=56 << 20),
    )(
        positions, strength, core_radius[None], dye_amount[None], cell_fraction, cell_index[None],
        tile_local[None], owner_dom.reshape(1, local),
    )


def solution(mesh):
    both = ("dom", "blk")
    placed = (P(None, both), P(None, both), P(both), P(both), P(None, both), P(both), P(both), P(both, None))
    return jax.shard_map(
        on_device,
        mesh=mesh,
        in_specs=placed,
        out_specs=(P(None, both), P(both, None, None)),
        check_vma=False,
    )
```

```python
import functools
import math

import jax
import jax.numpy as jnp
from jax import lax
from jax.experimental import pallas as pl
from jax.experimental.pallas import tpu as pltpu
from jax.sharding import PartitionSpec as P

MESH = pl.DeviceIdType.MESH
f32, bf16 = jnp.float32, jnp.bfloat16
kernel_scale = 1.0 / (4.0 * math.pi)


def cross_rows(u, v):
    return [u[1] * v[2] - u[2] * v[1], u[2] * v[0] - u[0] * v[2], u[0] * v[1] - u[1] * v[0]]


def split(value, parts):
    pieces = []
    for _ in range(parts):
        piece = value.astype(bf16)
        pieces.append(piece)
        value = value - piece.astype(f32)
    return pieces


def inner(u):
    return 1.0 - 2.5 * u * u + 1.5 * u * u * u


def outer(u):
    return 0.5 * (2.0 - u) * (2.0 - u) * (1.0 - u)


def axis_weights(base, nodes, cells):
    local = base.shape[1]
    ids = lax.broadcasted_iota(jnp.int32, (cells, local), 0)
    total = jnp.zeros((cells, local), f32)
    for node in range(4):
        total = total + jnp.where(((base + (node - 1)) & (cells - 1)) == ids, nodes[node], 0.0)
    return total


TT, ST, PIECE, CHUNK, UNROLL = 256, 512, 128, 32, 16


def stack_split(value, parts):
    return [piece.astype(f32) for piece in split(value, parts)]


def step_kernel(
    n_dom, n_blk, pos_ref, str_ref, rad_ref, dye_ref, frac_ref, cell_ref, tile_ref, owner_ref,
    vel_ref, grid_ref,
    blocks_ref, tgt_ref, src_ref, rk_ref, rg_ref, ok_ref, og_ref, q0, q1, part_ref, side_ref, both_ref, got_ref,
    blk_send, blk_recv, dom_send, dom_recv, near_send, near_recv,
):
    local = pos_ref.shape[1]
    dom, blk = lax.axis_index("dom"), lax.axis_index("blk")
    barrier = pltpu.get_barrier_semaphore()
    for step in range(1, n_blk):
        pl.semaphore_signal(barrier, inc=1, device_id={"blk": lax.rem(blk + step, n_blk)}, device_id_type=MESH)
    for step in range(2, n_dom, 2):
        pl.semaphore_signal(barrier, inc=1, device_id={"dom": lax.rem(dom + step, n_dom)}, device_id_type=MESH)
    pl.semaphore_signal(barrier, inc=1, device_id={"dom": dom + 1 - 2 * lax.rem(dom, 2)}, device_id_type=MESH)

    points = [pos_ref[i : i + 1, :] for i in range(3)]
    vortex = [str_ref[i : i + 1, :] for i in range(3)]
    radius = rad_ref[...]
    norm = points[0] * points[0] + points[1] * points[1] + points[2] * points[2]
    one, zero = jnp.ones_like(norm), jnp.zeros_like(norm)
    lead = [kernel_scale * row for row in vortex + cross_rows(vortex, points)]
    blocks_ref[0, 0:8, :] = jnp.concatenate(lead + [zero] * 2, 0)
    blocks_ref[0, 8:16, :] = jnp.concatenate(
        [-2.0 * row for row in points] + [norm + radius * radius, one] + [zero] * 3, 0
    )
    pl.semaphore_wait(barrier, n_blk - 1 + n_dom // 2)

    steps = list(range(2, n_blk, 2)) + list(range(1, n_blk, 2))
    blk_copies = []
    for slot, step in enumerate(steps, 1):
        copy = pltpu.make_async_remote_copy(
            src_ref=blocks_ref.at[0],
            dst_ref=blocks_ref.at[slot],
            send_sem=blk_send.at[slot],
            recv_sem=blk_recv.at[slot],
            device_id={"blk": lax.rem(blk + step, n_blk)},
            device_id_type=MESH,
        )
        copy.start()
        blk_copies.append(copy)

    t1, t2, t3 = stack_split(jnp.concatenate(points + [one, norm] + [zero] * 3, 0), 3)
    tgt_ref[...] = jnp.concatenate([t1, t2, t3, t1, t2, t1], 0).astype(bf16)
    ok_ref[...] = jnp.zeros_like(ok_ref)
    og_ref[...] = jnp.zeros_like(og_ref)

    qs = (q0, q1)
    chunks = local // ST
    count = chunks * (local // TT)
    halves = count // UNROLL

    def place_of(index):
        step = lax.rem(index, count)
        return (
            lax.rem(index // count, 2),
            pl.multiple_of(lax.rem(step, chunks) * ST, ST),
            pl.multiple_of(step // chunks * TT, TT),
        )

    def squares(index, slot, row):
        side, start, at = place_of(index)
        qs[slot][row : row + PIECE, :] = jnp.dot(
            src_ref[side, pl.ds(pl.multiple_of(start + row, PIECE), PIECE), :],
            tgt_ref[:, pl.ds(at, TT)],
            preferred_element_type=f32,
        )

    def values(slot, row, kern_parts, slope_parts):
        for at in range(row, row + PIECE, CHUNK):
            inverse = lax.rsqrt(qs[slot][at : at + CHUNK, :])
            second = inverse * inverse
            kern = second * inverse
            slope = kern * second
            kern_hi = kern.astype(bf16)
            slope_hi = slope.astype(bf16)
            kern_parts += [kern_hi, (kern - kern_hi.astype(f32)).astype(bf16)]
            slope_parts += [slope_hi, (slope - slope_hi.astype(f32)).astype(bf16)]

    def sums(index, kern_parts, slope_parts):
        side, start, at = place_of(index)
        twice = pl.ds(pl.multiple_of(2 * start, 2 * ST), 2 * ST)
        ok_ref[:, pl.ds(at, TT)] += jnp.dot(
            rk_ref[side, :, twice], jnp.concatenate(kern_parts, 0), preferred_element_type=f32
        )
        og_ref[:, pl.ds(at, TT)] += jnp.dot(
            rg_ref[side, :, twice], jnp.concatenate(slope_parts, 0), preferred_element_type=f32
        )

    column = lax.broadcasted_iota(jnp.int32, (128, 256), 1)
    origin = (column // (2 * CHUNK)) * CHUNK + column % CHUNK
    double = jnp.where(lax.broadcasted_iota(jnp.int32, (128, 256), 0) == origin, 1.0, 0.0).astype(bf16)

    def block_tables(block):
        side = lax.rem(block, 2)
        lead = blocks_ref[block, 0:8, :]
        place = blocks_ref[block, 8:16, :]
        groups = [split(lead if k == 0 else place[k - 1 : k, :] * lead, 2) for k in range(4)]
        rows = jnp.concatenate(
            [g.astype(f32) for g in groups[0]]
            + [g[0].astype(f32) for g in groups]
            + [g[1].astype(f32) for g in groups],
            0,
        ).astype(bf16)
        doubled = jnp.dot(
            jnp.concatenate([rows[:, at : at + 128] for at in range(0, local, 128)], 0),
            double,
            preferred_element_type=f32,
        ).astype(bf16)
        for k in range(local // 128):
            rk_ref[side, :, 256 * k : 256 * k + 256] = doubled[80 * k : 80 * k + 16]
            rg_ref[side, :, 256 * k : 256 * k + 256] = doubled[80 * k + 16 : 80 * k + 80]
        for at in range(0, local, 128):
            s1, s2, s3 = stack_split(place[:, at : at + 128], 3)
            src_ref[side, at : at + 128, :] = jnp.concatenate([s1, s1, s1, s2, s2, s3], 0).T.astype(bf16)

    block_tables(0)
    for row in range(0, ST, PIECE):
        squares(0, 0, row)

    @pl.loop(0, n_blk * halves)
    def _(part):
        block = part // halves + 1

        @pl.when((lax.rem(part, halves) == halves - 1) & (block < n_blk))
        def _():
            pltpu.make_async_remote_copy(
                src_ref=blocks_ref.at[0],
                dst_ref=blocks_ref.at[block],
                send_sem=blk_send.at[block],
                recv_sem=blk_recv.at[block],
                device_id={"blk": lax.rem(blk + 1, n_blk)},
                device_id_type=MESH,
            ).wait_recv()
            block_tables(block)

        for step in range(UNROLL):
            index = UNROLL * part + step
            slot = step % 2
            kern_parts, slope_parts = [], []
            for row in range(0, ST, PIECE):
                squares(jnp.minimum(index + 1, n_blk * count - 1), 1 - slot, row)
                values(slot, row, kern_parts, slope_parts)
            sums(index, kern_parts, slope_parts)

    for copy in blk_copies:
        copy.wait_send()

    first = ok_ref[0:8, :] + ok_ref[8:16, :]
    first = [first[i : i + 1, :] for i in range(6)]
    second = []
    for k in range(4):
        rows = og_ref[8 * k : 8 * k + 8, :] + og_ref[32 + 8 * k : 40 + 8 * k, :]
        second.append([rows[i : i + 1, :] for i in range(6)])
    turned = cross_rows(first[0:3], points)
    velocity = [turned[i] - first[3 + i] for i in range(3)]
    vel_ref[...] = jnp.concatenate(velocity, 0)
    term_one = cross_rows(first[0:3], vortex)
    dot_self = vortex[0] * points[0] + vortex[1] * points[1] + vortex[2] * points[2]
    mixed_one = [-0.5 * sum(vortex[k] * second[1 + k][i] for k in range(3)) for i in range(3)]
    mixed_two = [-0.5 * sum(vortex[k] * second[1 + k][3 + i] for k in range(3)) for i in range(3)]
    slope_turned = cross_rows(second[0][0:3], points)
    mixed_turned = cross_rows(mixed_one, points)
    carried = []
    for i in range(3):
        term_two = dot_self * (slope_turned[i] - second[0][3 + i]) - mixed_turned[i] + mixed_two[i]
        carried.append((vortex[i] + 0.02 * (term_one[i] - 3.0 * term_two)) * 32.0)
    carried.append(dye_ref[...] * 32.0)

    cell = cell_ref[...]
    starts = jnp.concatenate([cell & 7, (cell >> 3) & 3, cell >> 5], 0).astype(f32)
    coords = starts + frac_ref[...] + 2.0 * jnp.concatenate(velocity, 0)
    lowest = jnp.floor(coords)
    near = coords - lowest
    base = lowest.astype(jnp.int32)
    nodes = [outer(near + 1.0), inner(near), inner(1.0 - near), outer(2.0 - near)]
    weights = [
        axis_weights(base[i : i + 1, :], [node[i : i + 1, :] for node in nodes], 8 if i == 0 else 4)
        for i in range(3)
    ]
    plane = [weights[2][z : z + 1, :] * weights[1][y : y + 1, :] for z in range(4) for y in range(4)]

    tiles = grid_ref.shape[0]
    tile = owner_ref[...] * tiles + tile_ref[...]
    ids = lax.broadcasted_iota(jnp.int32, (n_dom * tiles, local), 0)
    onehot = jnp.where(ids == tile, 1.0, 0.0).astype(bf16)
    twice = jnp.concatenate([onehot, onehot], 1)
    core, chip, chips = lax.rem(dom, 2), dom // 2, n_dom // 2
    partner = dom + 1 - 2 * core
    near_copies, far_copies = [], []
    for pair in range(2):
        spread = jnp.concatenate(
            [weights[0] * (plane[k] * carried[2 * pair + c]) for c in range(2) for k in range(16)], 0
        )
        part = lax.dot_general(
            twice,
            jnp.concatenate(split(spread, 2), 1),
            (((1,), (1,)), ((), ())),
            preferred_element_type=f32,
        ).reshape(n_dom, tiles, 256)
        for owner in range(n_dom):
            part_ref[pair, owner % 2, owner // 2] = part[owner]
        copy = pltpu.make_async_remote_copy(
            src_ref=part_ref.at[pair, 1 - core],
            dst_ref=side_ref.at[pair],
            send_sem=near_send.at[pair],
            recv_sem=near_recv.at[pair],
            device_id={"dom": partner},
            device_id_type=MESH,
        )
        copy.start()
        near_copies.append(copy)
    for pair in range(2):
        near_copies[pair].wait_recv()
        both_ref[pair] = part_ref[pair, core] + side_ref[pair]
        for step in range(1, chips):
            peer = lax.rem(chip + step, chips)
            copy = pltpu.make_async_remote_copy(
                src_ref=both_ref.at[pair, peer],
                dst_ref=got_ref.at[pair, step],
                send_sem=dom_send.at[pair, step],
                recv_sem=dom_recv.at[pair, step],
                device_id={"dom": 2 * peer + core},
                device_id_type=MESH,
            )
            copy.start()
            far_copies.append(copy)
    for pair in range(2):
        for copy in far_copies[pair * (chips - 1) : (pair + 1) * (chips - 1)]:
            copy.wait_recv()
        total = both_ref[pair, chip]
        for step in range(1, chips):
            total = total + got_ref[pair, step]
        for c in range(2):
            grid_ref[:, 2 * pair + c, :] = total[:, 128 * c : 128 * c + 128]
    for copy in near_copies + far_copies:
        copy.wait_send()


def on_device(
    positions, strength, core_radius, dye_amount, cell_fraction, cell_index, tile_local, owner_dom
):
    n_dom, n_blk = lax.axis_size("dom"), lax.axis_size("blk")
    local = positions.shape[1]
    tiles = local // 128
    vmem = pl.BlockSpec(memory_space=pltpu.VMEM)
    return pl.pallas_call(
        functools.partial(step_kernel, n_dom, n_blk),
        out_shape=(
            jax.ShapeDtypeStruct((3, local), f32),
            jax.ShapeDtypeStruct((tiles, 4, 128), f32),
        ),
        in_specs=[vmem] * 8,
        out_specs=(vmem, vmem),
        scratch_shapes=[
            pltpu.VMEM((n_blk, 16, local), f32),
            pltpu.VMEM((48, local), bf16),
            pltpu.VMEM((2, local, 48), bf16),
            pltpu.VMEM((2, 16, 2 * local), bf16),
            pltpu.VMEM((2, 64, 2 * local), bf16),
            pltpu.VMEM((16, local), f32),
            pltpu.VMEM((64, local), f32),
        ]
        + [pltpu.VMEM((ST, TT), f32)] * 2
        + [pltpu.VMEM((2, 2, n_dom // 2, tiles, 256), f32)]
        + [pltpu.VMEM((2, n_dom // 2, tiles, 256), f32)] * 3
        + [pltpu.SemaphoreType.DMA((n_blk,))] * 2
        + [pltpu.SemaphoreType.DMA((2, n_dom // 2))] * 2
        + [pltpu.SemaphoreType.DMA((2,))] * 2,
        compiler_params=pltpu.CompilerParams(collective_id=0, has_side_effects=True, vmem_limit_bytes=56 << 20),
    )(
        positions, strength, core_radius[None], dye_amount[None], cell_fraction, cell_index[None],
        tile_local[None], owner_dom.reshape(1, local),
    )


def solution(mesh):
    both = ("dom", "blk")
    placed = (P(None, both), P(None, both), P(both), P(both), P(None, both), P(both), P(both), P(both, None))
    return jax.shard_map(
        on_device,
        mesh=mesh,
        in_specs=placed,
        out_specs=(P(None, both), P(both, None, None)),
        check_vma=False,
    )
```

```python
import functools
import math

import jax
import jax.numpy as jnp
from jax import lax
from jax.experimental import pallas as pl
from jax.experimental.pallas import tpu as pltpu
from jax.sharding import PartitionSpec as P

MESH = pl.DeviceIdType.MESH
f32, bf16 = jnp.float32, jnp.bfloat16
kernel_scale = 1.0 / (4.0 * math.pi)


def cross_rows(u, v):
    return [u[1] * v[2] - u[2] * v[1], u[2] * v[0] - u[0] * v[2], u[0] * v[1] - u[1] * v[0]]


def split(value, parts):
    pieces = []
    for _ in range(parts):
        piece = value.astype(bf16)
        pieces.append(piece)
        value = value - piece.astype(f32)
    return pieces


def inner(u):
    return 1.0 - 2.5 * u * u + 1.5 * u * u * u


def outer(u):
    return 0.5 * (2.0 - u) * (2.0 - u) * (1.0 - u)


def axis_weights(base, nodes, cells):
    local = base.shape[1]
    ids = lax.broadcasted_iota(jnp.int32, (cells, local), 0)
    total = jnp.zeros((cells, local), f32)
    for node in range(4):
        total = total + jnp.where(((base + (node - 1)) & (cells - 1)) == ids, nodes[node], 0.0)
    return total


TT, ST, PIECE, CHUNK = 256, 512, 128, 32


def stack_split(value, parts):
    return [piece.astype(f32) for piece in split(value, parts)]


def step_kernel(
    n_dom, n_blk, pos_ref, str_ref, rad_ref, dye_ref, frac_ref, cell_ref, tile_ref, owner_ref,
    vel_ref, grid_ref,
    blocks_ref, tgt_ref, src_ref, rk_ref, rg_ref, ok_ref, og_ref, q0, q1, part_ref, side_ref, both_ref, got_ref,
    blk_send, blk_recv, dom_send, dom_recv, near_send, near_recv,
):
    local = pos_ref.shape[1]
    dom, blk = lax.axis_index("dom"), lax.axis_index("blk")
    barrier = pltpu.get_barrier_semaphore()
    for step in range(1, n_blk):
        pl.semaphore_signal(barrier, inc=1, device_id={"blk": lax.rem(blk + step, n_blk)}, device_id_type=MESH)
    for step in range(2, n_dom, 2):
        pl.semaphore_signal(barrier, inc=1, device_id={"dom": lax.rem(dom + step, n_dom)}, device_id_type=MESH)
    pl.semaphore_signal(barrier, inc=1, device_id={"dom": dom + 1 - 2 * lax.rem(dom, 2)}, device_id_type=MESH)

    points = [pos_ref[i : i + 1, :] for i in range(3)]
    vortex = [str_ref[i : i + 1, :] for i in range(3)]
    radius = rad_ref[...]
    norm = points[0] * points[0] + points[1] * points[1] + points[2] * points[2]
    one, zero = jnp.ones_like(norm), jnp.zeros_like(norm)
    lead = [kernel_scale * row for row in vortex + cross_rows(vortex, points)]
    blocks_ref[0, 0:8, :] = jnp.concatenate(lead + [zero] * 2, 0)
    blocks_ref[0, 8:16, :] = jnp.concatenate(
        [-2.0 * row for row in points] + [norm + radius * radius, one] + [zero] * 3, 0
    )
    pl.semaphore_wait(barrier, n_blk - 1 + n_dom // 2)

    steps = list(range(2, n_blk, 2)) + list(range(1, n_blk, 2))
    blk_copies = []
    for slot, step in enumerate(steps, 1):
        copy = pltpu.make_async_remote_copy(
            src_ref=blocks_ref.at[0],
            dst_ref=blocks_ref.at[slot],
            send_sem=blk_send.at[slot],
            recv_sem=blk_recv.at[slot],
            device_id={"blk": lax.rem(blk + step, n_blk)},
            device_id_type=MESH,
        )
        copy.start()
        blk_copies.append(copy)

    t1, t2, t3 = stack_split(jnp.concatenate(points + [one, norm] + [zero] * 3, 0), 3)
    tgt_ref[...] = jnp.concatenate([t1, t2, t3, t1, t2, t1], 0).astype(bf16)
    ok_ref[...] = jnp.zeros_like(ok_ref)
    og_ref[...] = jnp.zeros_like(og_ref)

    qs = (q0, q1)
    chunks = local // ST
    count = chunks * (local // TT)

    def place_of(step):
        return step % chunks * ST, step // chunks * TT

    def squares(index, slot, row):
        start, at = place_of(index)
        qs[slot][row : row + PIECE, :] = jnp.dot(
            src_ref[start + row : start + row + PIECE, :],
            tgt_ref[:, at : at + TT],
            preferred_element_type=f32,
        )

    def values(slot, row, kern_parts, slope_parts):
        for at in range(row, row + PIECE, CHUNK):
            inverse = lax.rsqrt(qs[slot][at : at + CHUNK, :])
            second = inverse * inverse
            kern = second * inverse
            slope = kern * second
            kern_hi = kern.astype(bf16)
            slope_hi = slope.astype(bf16)
            kern_parts += [kern_hi, (kern - kern_hi.astype(f32)).astype(bf16)]
            slope_parts += [slope_hi, (slope - slope_hi.astype(f32)).astype(bf16)]

    def sums(index, kern_parts, slope_parts):
        start, at = place_of(index)
        twice = slice(2 * start, 2 * start + 2 * ST)
        ok_ref[:, at : at + TT] += jnp.dot(
            rk_ref[:, twice], jnp.concatenate(kern_parts, 0), preferred_element_type=f32
        )
        og_ref[:, at : at + TT] += jnp.dot(
            rg_ref[:, twice], jnp.concatenate(slope_parts, 0), preferred_element_type=f32
        )

    column = lax.broadcasted_iota(jnp.int32, (128, 256), 1)
    origin = (column // (2 * CHUNK)) * CHUNK + column % CHUNK
    double = jnp.where(lax.broadcasted_iota(jnp.int32, (128, 256), 0) == origin, 1.0, 0.0).astype(bf16)

    def block_tables(block):
        lead = blocks_ref[block, 0:8, :]
        place = blocks_ref[block, 8:16, :]
        groups = [split(lead if k == 0 else place[k - 1 : k, :] * lead, 2) for k in range(4)]
        rows = jnp.concatenate(
            [g.astype(f32) for g in groups[0]]
            + [g[0].astype(f32) for g in groups]
            + [g[1].astype(f32) for g in groups],
            0,
        ).astype(bf16)
        doubled = jnp.dot(
            jnp.concatenate([rows[:, at : at + 128] for at in range(0, local, 128)], 0),
            double,
            preferred_element_type=f32,
        ).astype(bf16)
        for k in range(local // 128):
            rk_ref[:, 256 * k : 256 * k + 256] = doubled[80 * k : 80 * k + 16]
            rg_ref[:, 256 * k : 256 * k + 256] = doubled[80 * k + 16 : 80 * k + 80]
        for at in range(0, local, 128):
            s1, s2, s3 = stack_split(place[:, at : at + 128], 3)
            src_ref[at : at + 128, :] = jnp.concatenate([s1, s1, s1, s2, s2, s3], 0).T.astype(bf16)

    @pl.loop(0, n_blk)
    def _(block):
        @pl.when(block > 0)
        def _():
            pltpu.make_async_remote_copy(
                src_ref=blocks_ref.at[0],
                dst_ref=blocks_ref.at[block],
                send_sem=blk_send.at[block],
                recv_sem=blk_recv.at[block],
                device_id={"blk": lax.rem(blk + 1, n_blk)},
                device_id_type=MESH,
            ).wait_recv()

        block_tables(block)
        for row in range(0, ST, PIECE):
            squares(0, 0, row)
        for index in range(count):
            slot = index % 2
            kern_parts, slope_parts = [], []
            for row in range(0, ST, PIECE):
                if index + 1 < count:
                    squares(index + 1, 1 - slot, row)
                values(slot, row, kern_parts, slope_parts)
            sums(index, kern_parts, slope_parts)

    for copy in blk_copies:
        copy.wait_send()

    first = ok_ref[0:8, :] + ok_ref[8:16, :]
    first = [first[i : i + 1, :] for i in range(6)]
    second = []
    for k in range(4):
        rows = og_ref[8 * k : 8 * k + 8, :] + og_ref[32 + 8 * k : 40 + 8 * k, :]
        second.append([rows[i : i + 1, :] for i in range(6)])
    turned = cross_rows(first[0:3], points)
    velocity = [turned[i] - first[3 + i] for i in range(3)]
    vel_ref[...] = jnp.concatenate(velocity, 0)
    term_one = cross_rows(first[0:3], vortex)
    dot_self = vortex[0] * points[0] + vortex[1] * points[1] + vortex[2] * points[2]
    mixed_one = [-0.5 * sum(vortex[k] * second[1 + k][i] for k in range(3)) for i in range(3)]
    mixed_two = [-0.5 * sum(vortex[k] * second[1 + k][3 + i] for k in range(3)) for i in range(3)]
    slope_turned = cross_rows(second[0][0:3], points)
    mixed_turned = cross_rows(mixed_one, points)
    carried = []
    for i in range(3):
        term_two = dot_self * (slope_turned[i] - second[0][3 + i]) - mixed_turned[i] + mixed_two[i]
        carried.append((vortex[i] + 0.02 * (term_one[i] - 3.0 * term_two)) * 32.0)
    carried.append(dye_ref[...] * 32.0)

    cell = cell_ref[...]
    starts = jnp.concatenate([cell & 7, (cell >> 3) & 3, cell >> 5], 0).astype(f32)
    coords = starts + frac_ref[...] + 2.0 * jnp.concatenate(velocity, 0)
    lowest = jnp.floor(coords)
    near = coords - lowest
    base = lowest.astype(jnp.int32)
    nodes = [outer(near + 1.0), inner(near), inner(1.0 - near), outer(2.0 - near)]
    weights = [
        axis_weights(base[i : i + 1, :], [node[i : i + 1, :] for node in nodes], 8 if i == 0 else 4)
        for i in range(3)
    ]
    plane = [weights[2][z : z + 1, :] * weights[1][y : y + 1, :] for z in range(4) for y in range(4)]

    tiles = grid_ref.shape[0]
    tile = owner_ref[...] * tiles + tile_ref[...]
    ids = lax.broadcasted_iota(jnp.int32, (n_dom * tiles, local), 0)
    onehot = jnp.where(ids == tile, 1.0, 0.0).astype(bf16)
    twice = jnp.concatenate([onehot, onehot], 1)
    core, chip, chips = lax.rem(dom, 2), dom // 2, n_dom // 2
    partner = dom + 1 - 2 * core
    near_copies, far_copies = [], []
    for pair in range(2):
        spread = jnp.concatenate(
            [weights[0] * (plane[k] * carried[2 * pair + c]) for c in range(2) for k in range(16)], 0
        )
        part = lax.dot_general(
            twice,
            jnp.concatenate(split(spread, 2), 1),
            (((1,), (1,)), ((), ())),
            preferred_element_type=f32,
        ).reshape(n_dom, tiles, 256)
        for owner in range(n_dom):
            part_ref[pair, owner % 2, owner // 2] = part[owner]
        copy = pltpu.make_async_remote_copy(
            src_ref=part_ref.at[pair, 1 - core],
            dst_ref=side_ref.at[pair],
            send_sem=near_send.at[pair],
            recv_sem=near_recv.at[pair],
            device_id={"dom": partner},
            device_id_type=MESH,
        )
        copy.start()
        near_copies.append(copy)
    for pair in range(2):
        near_copies[pair].wait_recv()
        both_ref[pair] = part_ref[pair, core] + side_ref[pair]
        for step in range(1, chips):
            peer = lax.rem(chip + step, chips)
            copy = pltpu.make_async_remote_copy(
                src_ref=both_ref.at[pair, peer],
                dst_ref=got_ref.at[pair, step],
                send_sem=dom_send.at[pair, step],
                recv_sem=dom_recv.at[pair, step],
                device_id={"dom": 2 * peer + core},
                device_id_type=MESH,
            )
            copy.start()
            far_copies.append(copy)
    for pair in range(2):
        for copy in far_copies[pair * (chips - 1) : (pair + 1) * (chips - 1)]:
            copy.wait_recv()
        total = both_ref[pair, chip]
        for step in range(1, chips):
            total = total + got_ref[pair, step]
        for c in range(2):
            grid_ref[:, 2 * pair + c, :] = total[:, 128 * c : 128 * c + 128]
    for copy in near_copies + far_copies:
        copy.wait_send()


def on_device(
    positions, strength, core_radius, dye_amount, cell_fraction, cell_index, tile_local, owner_dom
):
    n_dom, n_blk = lax.axis_size("dom"), lax.axis_size("blk")
    local = positions.shape[1]
    tiles = local // 128
    vmem = pl.BlockSpec(memory_space=pltpu.VMEM)
    return pl.pallas_call(
        functools.partial(step_kernel, n_dom, n_blk),
        out_shape=(
            jax.ShapeDtypeStruct((3, local), f32),
            jax.ShapeDtypeStruct((tiles, 4, 128), f32),
        ),
        in_specs=[vmem] * 8,
        out_specs=(vmem, vmem),
        scratch_shapes=[
            pltpu.VMEM((n_blk, 16, local), f32),
            pltpu.VMEM((48, local), bf16),
            pltpu.VMEM((local, 48), bf16),
            pltpu.VMEM((16, 2 * local), bf16),
            pltpu.VMEM((64, 2 * local), bf16),
            pltpu.VMEM((16, local), f32),
            pltpu.VMEM((64, local), f32),
        ]
        + [pltpu.VMEM((ST, TT), f32)] * 2
        + [pltpu.VMEM((2, 2, n_dom // 2, tiles, 256), f32)]
        + [pltpu.VMEM((2, n_dom // 2, tiles, 256), f32)] * 3
        + [pltpu.SemaphoreType.DMA((n_blk,))] * 2
        + [pltpu.SemaphoreType.DMA((2, n_dom // 2))] * 2
        + [pltpu.SemaphoreType.DMA((2,))] * 2,
        compiler_params=pltpu.CompilerParams(collective_id=0, has_side_effects=True, vmem_limit_bytes=56 << 20),
    )(
        positions, strength, core_radius[None], dye_amount[None], cell_fraction, cell_index[None],
        tile_local[None], owner_dom.reshape(1, local),
    )


def solution(mesh):
    both = ("dom", "blk")
    placed = (P(None, both), P(None, both), P(both), P(both), P(None, both), P(both), P(both), P(both, None))
    return jax.shard_map(
        on_device,
        mesh=mesh,
        in_specs=placed,
        out_specs=(P(None, both), P(both, None, None)),
        check_vma=False,
    )
```

```python
import functools
import math

import jax
import jax.numpy as jnp
from jax import lax
from jax.experimental import pallas as pl
from jax.experimental.pallas import tpu as pltpu
from jax.sharding import PartitionSpec as P

MESH = pl.DeviceIdType.MESH
f32, bf16 = jnp.float32, jnp.bfloat16
kernel_scale = 1.0 / (4.0 * math.pi)


def cross_rows(u, v):
    return [u[1] * v[2] - u[2] * v[1], u[2] * v[0] - u[0] * v[2], u[0] * v[1] - u[1] * v[0]]


def split(value, parts):
    pieces = []
    for _ in range(parts):
        piece = value.astype(bf16)
        pieces.append(piece)
        value = value - piece.astype(f32)
    return pieces


def inner(u):
    return 1.0 - 2.5 * u * u + 1.5 * u * u * u


def outer(u):
    return 0.5 * (2.0 - u) * (2.0 - u) * (1.0 - u)


def axis_weights(base, nodes, cells):
    local = base.shape[1]
    ids = lax.broadcasted_iota(jnp.int32, (cells, local), 0)
    total = jnp.zeros((cells, local), f32)
    for node in range(4):
        total = total + jnp.where(((base + (node - 1)) & (cells - 1)) == ids, nodes[node], 0.0)
    return total


TT, ST, PIECE, CHUNK = 256, 512, 128, 16


def stack_split(value, parts):
    return [piece.astype(f32) for piece in split(value, parts)]


def step_kernel(
    n_dom, n_blk, pos_ref, str_ref, rad_ref, dye_ref, frac_ref, cell_ref, tile_ref, owner_ref,
    vel_ref, grid_ref,
    blocks_ref, tgt_ref, src_ref, rk_ref, rg_ref, ok_ref, og_ref, q0, q1, part_ref, side_ref, both_ref, got_ref,
    blk_send, blk_recv, dom_send, dom_recv, near_send, near_recv,
):
    local = pos_ref.shape[1]
    dom, blk = lax.axis_index("dom"), lax.axis_index("blk")
    barrier = pltpu.get_barrier_semaphore()
    for step in range(1, n_blk):
        pl.semaphore_signal(barrier, inc=1, device_id={"blk": lax.rem(blk + step, n_blk)}, device_id_type=MESH)
    for step in range(2, n_dom, 2):
        pl.semaphore_signal(barrier, inc=1, device_id={"dom": lax.rem(dom + step, n_dom)}, device_id_type=MESH)
    pl.semaphore_signal(barrier, inc=1, device_id={"dom": dom + 1 - 2 * lax.rem(dom, 2)}, device_id_type=MESH)

    points = [pos_ref[i : i + 1, :] for i in range(3)]
    vortex = [str_ref[i : i + 1, :] for i in range(3)]
    radius = rad_ref[...]
    norm = points[0] * points[0] + points[1] * points[1] + points[2] * points[2]
    one, zero = jnp.ones_like(norm), jnp.zeros_like(norm)
    lead = [kernel_scale * row for row in vortex + cross_rows(vortex, points)]
    blocks_ref[0, 0:8, :] = jnp.concatenate(lead + [zero] * 2, 0)
    blocks_ref[0, 8:16, :] = jnp.concatenate(
        [-2.0 * row for row in points] + [norm + radius * radius, one] + [zero] * 3, 0
    )
    pl.semaphore_wait(barrier, n_blk - 1 + n_dom // 2)

    steps = list(range(2, n_blk, 2)) + list(range(1, n_blk, 2))
    blk_copies = []
    for slot, step in enumerate(steps, 1):
        copy = pltpu.make_async_remote_copy(
            src_ref=blocks_ref.at[0],
            dst_ref=blocks_ref.at[slot],
            send_sem=blk_send.at[slot],
            recv_sem=blk_recv.at[slot],
            device_id={"blk": lax.rem(blk + step, n_blk)},
            device_id_type=MESH,
        )
        copy.start()
        blk_copies.append(copy)

    t1, t2, t3 = stack_split(jnp.concatenate(points + [one, norm] + [zero] * 3, 0), 3)
    tgt_ref[...] = jnp.concatenate([t1, t2, t3, t1, t2, t1], 0).astype(bf16)
    ok_ref[...] = jnp.zeros_like(ok_ref)
    og_ref[...] = jnp.zeros_like(og_ref)

    qs = (q0, q1)
    chunks = local // ST
    count = chunks * (local // TT)

    def place_of(step):
        return step % chunks * ST, step // chunks * TT

    def squares(index, slot, row):
        start, at = place_of(index)
        qs[slot][row : row + PIECE, :] = jnp.dot(
            src_ref[start + row : start + row + PIECE, :],
            tgt_ref[:, at : at + TT],
            preferred_element_type=f32,
        )

    def values(slot, row, kern_parts, slope_parts):
        for at in range(row, row + PIECE, CHUNK):
            inverse = lax.rsqrt(qs[slot][at : at + CHUNK, :])
            second = inverse * inverse
            kern = second * inverse
            slope = kern * second
            kern_hi = kern.astype(bf16)
            slope_hi = slope.astype(bf16)
            kern_parts += [kern_hi, (kern - kern_hi.astype(f32)).astype(bf16)]
            slope_parts += [slope_hi, (slope - slope_hi.astype(f32)).astype(bf16)]

    def sums(index, kern_parts, slope_parts):
        start, at = place_of(index)
        twice = slice(2 * start, 2 * start + 2 * ST)
        ok_ref[:, at : at + TT] += jnp.dot(
            rk_ref[:, twice], jnp.concatenate(kern_parts, 0), preferred_element_type=f32
        )
        og_ref[:, at : at + TT] += jnp.dot(
            rg_ref[:, twice], jnp.concatenate(slope_parts, 0), preferred_element_type=f32
        )

    column = lax.broadcasted_iota(jnp.int32, (128, 256), 1)
    origin = (column // (2 * CHUNK)) * CHUNK + column % CHUNK
    double = jnp.where(lax.broadcasted_iota(jnp.int32, (128, 256), 0) == origin, 1.0, 0.0).astype(bf16)

    def block_tables(block):
        lead = blocks_ref[block, 0:8, :]
        place = blocks_ref[block, 8:16, :]
        groups = [split(lead if k == 0 else place[k - 1 : k, :] * lead, 2) for k in range(4)]
        rows = jnp.concatenate(
            [g.astype(f32) for g in groups[0]]
            + [g[0].astype(f32) for g in groups]
            + [g[1].astype(f32) for g in groups],
            0,
        ).astype(bf16)
        doubled = jnp.dot(
            jnp.concatenate([rows[:, at : at + 128] for at in range(0, local, 128)], 0),
            double,
            preferred_element_type=f32,
        ).astype(bf16)
        for k in range(local // 128):
            rk_ref[:, 256 * k : 256 * k + 256] = doubled[80 * k : 80 * k + 16]
            rg_ref[:, 256 * k : 256 * k + 256] = doubled[80 * k + 16 : 80 * k + 80]
        for at in range(0, local, 128):
            s1, s2, s3 = stack_split(place[:, at : at + 128], 3)
            src_ref[at : at + 128, :] = jnp.concatenate([s1, s1, s1, s2, s2, s3], 0).T.astype(bf16)

    @pl.loop(0, n_blk)
    def _(block):
        @pl.when(block > 0)
        def _():
            pltpu.make_async_remote_copy(
                src_ref=blocks_ref.at[0],
                dst_ref=blocks_ref.at[block],
                send_sem=blk_send.at[block],
                recv_sem=blk_recv.at[block],
                device_id={"blk": lax.rem(blk + 1, n_blk)},
                device_id_type=MESH,
            ).wait_recv()

        block_tables(block)
        for row in range(0, ST, PIECE):
            squares(0, 0, row)
        for index in range(count):
            slot = index % 2
            kern_parts, slope_parts = [], []
            for row in range(0, ST, PIECE):
                if index + 1 < count:
                    squares(index + 1, 1 - slot, row)
                values(slot, row, kern_parts, slope_parts)
            sums(index, kern_parts, slope_parts)

    for copy in blk_copies:
        copy.wait_send()

    first = ok_ref[0:8, :] + ok_ref[8:16, :]
    first = [first[i : i + 1, :] for i in range(6)]
    second = []
    for k in range(4):
        rows = og_ref[8 * k : 8 * k + 8, :] + og_ref[32 + 8 * k : 40 + 8 * k, :]
        second.append([rows[i : i + 1, :] for i in range(6)])
    turned = cross_rows(first[0:3], points)
    velocity = [turned[i] - first[3 + i] for i in range(3)]
    vel_ref[...] = jnp.concatenate(velocity, 0)
    term_one = cross_rows(first[0:3], vortex)
    dot_self = vortex[0] * points[0] + vortex[1] * points[1] + vortex[2] * points[2]
    mixed_one = [-0.5 * sum(vortex[k] * second[1 + k][i] for k in range(3)) for i in range(3)]
    mixed_two = [-0.5 * sum(vortex[k] * second[1 + k][3 + i] for k in range(3)) for i in range(3)]
    slope_turned = cross_rows(second[0][0:3], points)
    mixed_turned = cross_rows(mixed_one, points)
    carried = []
    for i in range(3):
        term_two = dot_self * (slope_turned[i] - second[0][3 + i]) - mixed_turned[i] + mixed_two[i]
        carried.append((vortex[i] + 0.02 * (term_one[i] - 3.0 * term_two)) * 32.0)
    carried.append(dye_ref[...] * 32.0)

    cell = cell_ref[...]
    starts = jnp.concatenate([cell & 7, (cell >> 3) & 3, cell >> 5], 0).astype(f32)
    coords = starts + frac_ref[...] + 2.0 * jnp.concatenate(velocity, 0)
    lowest = jnp.floor(coords)
    near = coords - lowest
    base = lowest.astype(jnp.int32)
    nodes = [outer(near + 1.0), inner(near), inner(1.0 - near), outer(2.0 - near)]
    weights = [
        axis_weights(base[i : i + 1, :], [node[i : i + 1, :] for node in nodes], 8 if i == 0 else 4)
        for i in range(3)
    ]
    plane = [weights[2][z : z + 1, :] * weights[1][y : y + 1, :] for z in range(4) for y in range(4)]

    tiles = grid_ref.shape[0]
    tile = owner_ref[...] * tiles + tile_ref[...]
    ids = lax.broadcasted_iota(jnp.int32, (n_dom * tiles, local), 0)
    onehot = jnp.where(ids == tile, 1.0, 0.0).astype(bf16)
    twice = jnp.concatenate([onehot, onehot], 1)
    core, chip, chips = lax.rem(dom, 2), dom // 2, n_dom // 2
    partner = dom + 1 - 2 * core
    near_copies, far_copies = [], []
    for pair in range(2):
        spread = jnp.concatenate(
            [weights[0] * (plane[k] * carried[2 * pair + c]) for c in range(2) for k in range(16)], 0
        )
        part = lax.dot_general(
            twice,
            jnp.concatenate(split(spread, 2), 1),
            (((1,), (1,)), ((), ())),
            preferred_element_type=f32,
        ).reshape(n_dom, tiles, 256)
        for owner in range(n_dom):
            part_ref[pair, owner % 2, owner // 2] = part[owner]
        copy = pltpu.make_async_remote_copy(
            src_ref=part_ref.at[pair, 1 - core],
            dst_ref=side_ref.at[pair],
            send_sem=near_send.at[pair],
            recv_sem=near_recv.at[pair],
            device_id={"dom": partner},
            device_id_type=MESH,
        )
        copy.start()
        near_copies.append(copy)
    for pair in range(2):
        near_copies[pair].wait_recv()
        both_ref[pair] = part_ref[pair, core] + side_ref[pair]
        for step in range(1, chips):
            peer = lax.rem(chip + step, chips)
            copy = pltpu.make_async_remote_copy(
                src_ref=both_ref.at[pair, peer],
                dst_ref=got_ref.at[pair, step],
                send_sem=dom_send.at[pair, step],
                recv_sem=dom_recv.at[pair, step],
                device_id={"dom": 2 * peer + core},
                device_id_type=MESH,
            )
            copy.start()
            far_copies.append(copy)
    for pair in range(2):
        for copy in far_copies[pair * (chips - 1) : (pair + 1) * (chips - 1)]:
            copy.wait_recv()
        total = both_ref[pair, chip]
        for step in range(1, chips):
            total = total + got_ref[pair, step]
        for c in range(2):
            grid_ref[:, 2 * pair + c, :] = total[:, 128 * c : 128 * c + 128]
    for copy in near_copies + far_copies:
        copy.wait_send()


def on_device(
    positions, strength, core_radius, dye_amount, cell_fraction, cell_index, tile_local, owner_dom
):
    n_dom, n_blk = lax.axis_size("dom"), lax.axis_size("blk")
    local = positions.shape[1]
    tiles = local // 128
    vmem = pl.BlockSpec(memory_space=pltpu.VMEM)
    return pl.pallas_call(
        functools.partial(step_kernel, n_dom, n_blk),
        out_shape=(
            jax.ShapeDtypeStruct((3, local), f32),
            jax.ShapeDtypeStruct((tiles, 4, 128), f32),
        ),
        in_specs=[vmem] * 8,
        out_specs=(vmem, vmem),
        scratch_shapes=[
            pltpu.VMEM((n_blk, 16, local), f32),
            pltpu.VMEM((48, local), bf16),
            pltpu.VMEM((local, 48), bf16),
            pltpu.VMEM((16, 2 * local), bf16),
            pltpu.VMEM((64, 2 * local), bf16),
            pltpu.VMEM((16, local), f32),
            pltpu.VMEM((64, local), f32),
        ]
        + [pltpu.VMEM((ST, TT), f32)] * 2
        + [pltpu.VMEM((2, 2, n_dom // 2, tiles, 256), f32)]
        + [pltpu.VMEM((2, n_dom // 2, tiles, 256), f32)] * 3
        + [pltpu.SemaphoreType.DMA((n_blk,))] * 2
        + [pltpu.SemaphoreType.DMA((2, n_dom // 2))] * 2
        + [pltpu.SemaphoreType.DMA((2,))] * 2,
        compiler_params=pltpu.CompilerParams(collective_id=0, has_side_effects=True, vmem_limit_bytes=56 << 20),
    )(
        positions, strength, core_radius[None], dye_amount[None], cell_fraction, cell_index[None],
        tile_local[None], owner_dom.reshape(1, local),
    )


def solution(mesh):
    both = ("dom", "blk")
    placed = (P(None, both), P(None, both), P(both), P(both), P(None, both), P(both), P(both), P(both, None))
    return jax.shard_map(
        on_device,
        mesh=mesh,
        in_specs=placed,
        out_specs=(P(None, both), P(both, None, None)),
        check_vma=False,
    )
```
